32 devices in a mesh: parts: 2 (over x), blk: 16 (over z, y, core).
Axes of the slice: x: 2, y: 2, z: 4, core: 2. Of those that a mesh axis runs over, the one named last changes fastest.
Arguments:
- particles: bfloat16 [256, 2, 2048], P(('parts', 'blk')), parts along dimension 0, may hold values from -56 to 56, as said below
- offsets: int32 [2, 256], P(None, ('parts', 'blk')), parts along dimension 1, may hold values from -2 to 2
- references: bfloat16 [128, 2, 2048], P(('parts', 'blk')), parts along dimension 0, may hold values from -4 to 4, as said below
- inv_noise: float32 [32], replicated, may hold values from 0.01 to 0.04
- counts: int32 [32], P('parts'), parts along dimension 0, may hold values from 1 to 8, 48 in all
Outputs:
- loglik: float32 [256], P(('parts', 'blk')), parts along dimension 0
- class_sums: float32 [128, 2, 2048], P(('parts', 'blk')), parts along dimension 0
The draws below stay inside these ranges and needn't reach their ends.
There are 2 independent parts, one for each index of `parts`. The reference program is written for one: setup_inputs(seed, part) draws one part's arguments, and reference() takes and returns one part's arrays. A program takes and returns all parts, laid end to end along the dimension named above; an argument that names none is the same for every part. Nothing has to cross between parts.
Inputs may be any that keep to these rules, and one draw needn't show every extreme that they name: The particles of blk index d fill its first counts[d] slots; the counts sum to 48 and the largest is 8. `particles`: particle coefficients; slots beyond a device's count hold values that no output reads. `references`: class reference coefficients.
All inputs are finite; a program needn't handle non-finite values.
Results may differ from the reference program's by a relative error of at most 0.0075.
Values may be sent and summed in bfloat16 or wider, within the bound.
No kernel may reach another device: no remote copies, remote signals or barrier semaphores. Data moves between devices by JAX's collectives and lax.ppermute only.
A program may use at most 64 MiB of HBM per device.

```python
import math
import jax
import jax.numpy as jnp
import numpy as np
from jax import lax

CAP = 8
RADIAL_CYCLES = 32
POLAR_ANGLES = 64
SHIFT = 5
TRANS = 25
MEAN = 3
TOTAL = 48
SLOT_TOTAL = 128
CLASSES = 64
N_BLK = 16


def shared_references(key):
    base_key = jax.random.fold_in(key, 11)
    complete_shape = (CLASSES, 2, RADIAL_CYCLES, POLAR_ANGLES)
    return jax.random.truncated_normal(base_key, -4.0, 4.0, complete_shape, jnp.float32)


def draw_references(key, part):
    return shared_references(key).reshape(CLASSES, 2, RADIAL_CYCLES * POLAR_ANGLES).astype(jnp.bfloat16)


def draw_particles(key, part):
    base_key = jax.random.fold_in(key, 23)
    complete_shape = (SLOT_TOTAL, 2, RADIAL_CYCLES, POLAR_ANGLES)
    value_entries = jax.random.truncated_normal(base_key, -4.0, 4.0, complete_shape, jnp.float32)
    return value_entries.reshape(SLOT_TOTAL, 2, RADIAL_CYCLES * POLAR_ANGLES).astype(jnp.bfloat16)


def plant(array, own_key, smallest, top_value):
    shape = array.shape
    spot = [jax.random.randint(jax.random.fold_in(own_key, axis), (), 0, shape[axis]) for axis in range(len(shape))]
    array = array.at[tuple(spot)].set(smallest)
    longest = shape.index(max(shape))
    spot[longest] = (spot[longest] + 1) % shape[longest]
    return array.at[tuple(spot)].set(top_value)


def profile(number_of, total, reach, slope):
    weights = [(1 << 20) // math.isqrt(standing ** slope) + 1 for standing in range(2, number_of + 1)]
    rest, given = total - reach - (number_of - 1), [1] * (number_of - 1)
    while rest > 0:
        movable = [i for i in range(number_of - 1) if given[i] < reach]
        whole, budget = sum([weights[i] for i in movable]), rest
        for i in movable:
            more = min(reach - given[i], max(1, budget * weights[i] // whole), rest)
            given[i] = given[i] + more
            rest = rest - more
    return np.array([reach] + given)


def ragged_sizes(key, count, total, bound, lean):
    if count == 2:
        one = jax.random.randint(key, (), max(1, total - bound), min(bound, total - 1) + 1)
        return jnp.stack([one, total - one])
    tallies = jnp.asarray(profile(count, total, bound, lean), jnp.int32)
    pairs = (count - 1) // 2
    donor, taker = tallies[1:1 + 2 * pairs:2], tallies[2:2 + 2 * pairs:2]
    slack = jnp.minimum(donor - 1, bound - taker)
    passed = jax.random.randint(jax.random.fold_in(key, 1), (pairs,), 0, 1 << 20) % (slack + 1)
    tallies = tallies.at[1:1 + 2 * pairs:2].set(donor - passed).at[2:2 + 2 * pairs:2].set(taker + passed)
    return tallies[jax.random.permutation(jax.random.fold_in(key, 2), count)]


def setup_inputs(seed: int = 0, part: int = 0) -> dict:
    arg_keys = jax.random.split(jax.random.key(seed), 6)
    part_splits = jax.random.split(jax.random.fold_in(arg_keys[5], part), 6)
    particles = draw_particles(jax.random.fold_in(jax.random.fold_in(arg_keys[5], part), 71), part)
    offsets = plant(jax.random.randint(part_splits[1], (2, SLOT_TOTAL), -2, 3), jax.random.fold_in(part_splits[1], 1), -2, 2).astype(jnp.int32)
    references = draw_references(jax.random.fold_in(jax.random.fold_in(arg_keys[5], part), 71), part)
    inv_noise = jnp.clip(jnp.exp(jax.random.uniform(arg_keys[3], (RADIAL_CYCLES,), jnp.float32, math.log(0.01), math.log(0.04))), 0.01, 0.04)
    counts = ragged_sizes(part_splits[4], N_BLK, TOTAL, CAP, 2).astype(jnp.int32)
    return {"particles": particles, "offsets": offsets, "references": references, "inv_noise": inv_noise, "counts": counts}


def angle_tables(angles):
    angle_index = jnp.arange(angles, dtype=jnp.int32)
    product_terms = (angle_index[:, None] * angle_index[None, :]) % angles
    radians = product_terms.astype(jnp.float32) * (2.0 * math.pi / angles)
    return jnp.cos(radians), jnp.sin(radians)


def particle_spectra(slots_in, shifts, span_side, cycle_count, angles):
    particle_count = slots_in.shape[0]
    highest_score = lax.Precision.HIGHEST
    cosine_table, sine_table = angle_tables(angles)
    polar_angle = jnp.arange(angles, dtype=jnp.float32) * (2.0 * math.pi / angles)
    radius = jnp.arange(1, cycle_count + 1, dtype=jnp.float32)
    step_index = jnp.arange(span_side * span_side, dtype=jnp.int32)
    step_x = (step_index // span_side - span_side // 2).astype(jnp.float32)
    step_y = (step_index % span_side - span_side // 2).astype(jnp.float32)
    shift_x = shifts[0][:, None] + step_x[None, :]
    shift_y = shifts[1][:, None] + step_y[None, :]
    along_ray = shift_x[:, :, None] * jnp.cos(polar_angle) + shift_y[:, :, None] * jnp.sin(polar_angle)
    phases = (2.0 * math.pi / 128.0) * radius[None, None, :, None] * along_ray[:, :, None, :]
    slots_grid = slots_in.reshape(particle_count, 2, cycle_count, angles).astype(jnp.float32)
    real_in = slots_grid[:, 0][:, None]
    imag_in = slots_grid[:, 1][:, None]
    cos_phase = jnp.cos(phases)
    sin_phase = jnp.sin(phases)
    real_y = real_in * cos_phase + imag_in * sin_phase
    imag_y = imag_in * cos_phase - real_in * sin_phase
    real_hat = jnp.einsum("ptja,am->mjpt", real_y, cosine_table, precision=highest_score) + jnp.einsum("ptja,am->mjpt", imag_y, sine_table, precision=highest_score)
    imag_hat = jnp.einsum("ptja,am->mjpt", imag_y, cosine_table, precision=highest_score) - jnp.einsum("ptja,am->mjpt", real_y, sine_table, precision=highest_score)
    stacked = jnp.concatenate([real_hat, imag_hat], axis=1)
    return stacked.reshape(angles, 2 * cycle_count, particle_count * span_side * span_side).astype(jnp.bfloat16)


def reference_spectra(refs_in, inv_noise, cycle_count, angles):
    highest_score = lax.Precision.HIGHEST
    cosine_table, sine_table = angle_tables(angles)
    refs_grid = refs_in.reshape(refs_in.shape[0], 2, cycle_count, angles).astype(jnp.float32)
    real_in = refs_grid[:, 0]
    imag_in = refs_grid[:, 1]
    real_hat = jnp.einsum("cja,am->cjm", real_in, cosine_table, precision=highest_score) + jnp.einsum("cja,am->cjm", imag_in, sine_table, precision=highest_score)
    imag_hat = jnp.einsum("cja,am->cjm", imag_in, cosine_table, precision=highest_score) - jnp.einsum("cja,am->cjm", real_in, sine_table, precision=highest_score)
    weight = inv_noise[None, :, None]
    stacked = jnp.stack([real_hat * weight, imag_hat * weight], axis=1)
    return stacked.reshape(refs_in.shape[0], 2 * cycle_count * angles).astype(jnp.bfloat16)


def block_scores(particle_hat, class_block, inverse_total, cycle_count, angles):
    highest_score = lax.Precision.HIGHEST
    block_size = class_block.shape[0]
    spectra = class_block.reshape(block_size, 2, cycle_count, angles).astype(jnp.float32)
    left_mats = jnp.concatenate([spectra[:, 0], spectra[:, 1]], axis=1)
    right_mats = jnp.concatenate([-spectra[:, 1], spectra[:, 0]], axis=1)
    both_mats = jnp.concatenate([left_mats, right_mats], axis=0)
    product_terms = jnp.einsum("mkx,ckm->mcx", particle_hat.astype(jnp.float32), both_mats, precision=highest_score)
    product_terms = product_terms.reshape(angles, 2, block_size, product_terms.shape[-1])
    return jnp.einsum("zesn,ezp->psn", product_terms, inverse_total, precision=highest_score)


def class_images(class_spectra, cycle_count, angles):
    highest_score = lax.Precision.HIGHEST
    cosine_table, sine_table = angle_tables(angles)
    spectra = class_spectra.reshape(class_spectra.shape[0], 2, cycle_count, angles)
    real_acc = spectra[:, 0]
    imag_acc = spectra[:, 1]
    out_real = (jnp.einsum("cjm,mb->cjb", real_acc, cosine_table, precision=highest_score) - jnp.einsum("cjm,mb->cjb", imag_acc, sine_table, precision=highest_score)) / angles
    out_imag = (jnp.einsum("cjm,mb->cjb", real_acc, sine_table, precision=highest_score) + jnp.einsum("cjm,mb->cjb", imag_acc, cosine_table, precision=highest_score)) / angles
    return jnp.stack([out_real, out_imag], axis=1).reshape(class_spectra.shape[0], 2, cycle_count * angles)


def reference(particles, offsets, references, inv_noise, counts):
    highest_score = lax.Precision.HIGHEST
    cosine_table, sine_table = angle_tables(POLAR_ANGLES)
    inverse_total = jnp.stack([cosine_table / POLAR_ANGLES, -sine_table / POLAR_ANGLES])
    forward = jnp.stack([cosine_table, sine_table])
    spectra = reference_spectra(references, inv_noise, RADIAL_CYCLES, POLAR_ANGLES)
    count_ends = jnp.cumsum(counts).astype(jnp.int32)
    count_starts = (count_ends - counts).astype(jnp.int32)
    global_rank = jnp.arange(TOTAL, dtype=jnp.int32)
    owner_dev = jnp.sum((count_ends[None, :] <= global_rank[:, None]).astype(jnp.int32), axis=1)
    source = (owner_dev * CAP + global_rank - count_starts[owner_dev]).astype(jnp.int32)
    chosen = particles[source]
    shifts = offsets[:, source].astype(jnp.float32)
    group_size = 4 * MEAN
    chosen_blocks = chosen.reshape(TOTAL // group_size, group_size, 2, RADIAL_CYCLES * POLAR_ANGLES)
    shift_blocks = jnp.transpose(shifts.reshape(2, TOTAL // group_size, group_size), (1, 0, 2))

    def advance(running, block_item):
        block_slots, block_shifts = block_item
        particle_hat = particle_spectra(block_slots, block_shifts, SHIFT, RADIAL_CYCLES, POLAR_ANGLES)
        scores = block_scores(particle_hat, spectra, inverse_total, RADIAL_CYCLES, POLAR_ANGLES)
        score_grid = scores.reshape(POLAR_ANGLES, CLASSES, group_size, TRANS)
        peak_score = jnp.max(score_grid, axis=(0, 1, 3))
        block_liks = peak_score + jnp.log(jnp.sum(jnp.exp(score_grid - peak_score[None, None, :, None]), axis=(0, 1, 3)))
        row_loglik = jnp.repeat(block_liks, TRANS)
        posterior = jnp.exp(scores - row_loglik[None, None, :])
        weight_hat = jnp.einsum("rcx,grm->gmcx", posterior, forward, precision=highest_score).astype(jnp.bfloat16)
        mixed_sums = jnp.einsum("mkx,gmcx->mgck", particle_hat.astype(jnp.float32), weight_hat.astype(jnp.float32), precision=highest_score)
        real_acc = mixed_sums[:, 0, :, :RADIAL_CYCLES] - mixed_sums[:, 1, :, RADIAL_CYCLES:]
        imag_acc = mixed_sums[:, 0, :, RADIAL_CYCLES:] + mixed_sums[:, 1, :, :RADIAL_CYCLES]
        class_term = jnp.transpose(jnp.stack([real_acc, imag_acc], axis=0), (2, 0, 3, 1))
        return running + class_term, block_liks

    start_sums = jnp.zeros((CLASSES, 2, RADIAL_CYCLES, POLAR_ANGLES), jnp.float32)
    class_spectra, block_liks = lax.scan(advance, start_sums, (chosen_blocks, shift_blocks))
    class_sums = class_images(class_spectra.reshape(CLASSES, 2 * RADIAL_CYCLES * POLAR_ANGLES), RADIAL_CYCLES, POLAR_ANGLES)
    slot_position_index = jnp.arange(SLOT_TOTAL, dtype=jnp.int32)
    slot_dev = (slot_position_index // CAP).astype(jnp.int32)
    slot_pos = (slot_position_index % CAP).astype(jnp.int32)
    valid_slot_mask = slot_pos < counts[slot_dev]
    packed_scores = jnp.clip(count_starts[slot_dev] + slot_pos, 0, TOTAL - 1).astype(jnp.int32)
    flattened_likelihoods = block_liks.reshape(TOTAL)
    loglik = jnp.where(valid_slot_mask, flattened_likelihoods[packed_scores], jnp.zeros((SLOT_TOTAL,), jnp.float32))
    return (loglik, class_sums)
```

```python
import functools
import math

import jax
import jax.numpy as jnp
import numpy as np
from jax import lax
from jax.experimental import pallas as pl
from jax.experimental.pallas import tpu as pltpu
from jax.sharding import PartitionSpec as P

ANGLES = 64
SHIFT = 5
STEPS = SHIFT * SHIFT
MEAN = 3
CHUNK = 48
ROWS = STEPS * CHUNK
PAIR = 4 * ANGLES
F32 = jnp.float32
BF16 = jnp.bfloat16
VMEM_LIMIT = 60 * 1024 * 1024


def split(table, terms):
    rest = np.asarray(table, np.float64)
    out = []
    for _ in range(terms):
        piece = rest.astype(np.float32).astype(jnp.bfloat16)
        out.append(piece)
        rest = rest - piece.astype(np.float64)
    return out


def angle_products():
    index = np.arange(ANGLES)
    radians = 2.0 * math.pi / ANGLES * (index[:, None] * index[None, :] % ANGLES)
    return np.cos(radians), np.sin(radians)


def step_phases(cycles):
    polar = 2.0 * math.pi / ANGLES * np.arange(ANGLES)
    radius = np.arange(1, cycles + 1)
    step = np.arange(STEPS)
    along = (step // SHIFT - SHIFT // 2)[:, None] * np.cos(polar) + (step % SHIFT - SHIFT // 2)[
        :, None
    ] * np.sin(polar)
    phases = 2.0 * math.pi / 128.0 * radius[None, :, None] * along[:, None, :]
    return np.cos(phases), np.sin(phases)


def step_tables(cycles):
    cosine, sine = step_phases(cycles)
    tc = np.concatenate([cosine, cosine], axis=2).reshape(STEPS, -1).astype(np.float32)
    ts = np.concatenate([sine, -sine], axis=2).reshape(STEPS, -1).astype(np.float32)
    return tc, ts


def offset_table(cycles):
    cosine, sine = step_phases(cycles)
    both = np.concatenate([cosine.reshape(STEPS, -1), sine.reshape(STEPS, -1)], axis=1)
    both = np.pad(both, ((0, 32 - STEPS), (0, 0)))
    return np.concatenate(split(both, 3), axis=0)


def forward_matrix():
    cosine, sine = angle_products()
    return np.block([[cosine, -sine], [sine, cosine]])


def forward_stack():
    high, low = split(forward_matrix(), 2)
    return np.block([[high, low], [high, np.zeros_like(low)]])


def rotation_tables():
    cosine, sine = angle_products()
    cosine, sine = cosine / ANGLES, sine / ANGLES
    return (
        np.concatenate([cosine, cosine], axis=1).astype(np.float32),
        np.concatenate([sine, -sine], axis=1).astype(np.float32),
    )


def gather_tables():
    cosine, sine = angle_products()
    return (
        np.concatenate([cosine] * 4, axis=1).astype(np.float32),
        np.concatenate([sine] * 4, axis=1).astype(np.float32),
    )


def image_stack():
    cosine, sine = angle_products()
    table = np.zeros((2, 2, ANGLES, 2, 2, ANGLES))
    for parity in range(2):
        table[parity, 0, :, 0, parity] = cosine / ANGLES
        table[parity, 1, :, 0, parity] = -sine / ANGLES
        table[parity, 0, :, 1, parity] = sine / ANGLES
        table[parity, 1, :, 1, parity] = cosine / ANGLES
    high, low = split(table.reshape(PAIR, PAIR), 2)
    return np.concatenate([high, low], axis=1)


def dot(left, right, dims=((1,), (0,))):
    return lax.dot_general(left, right, (dims, ((), ())), preferred_element_type=F32)


def halves(value):
    high = value.astype(BF16)
    return high, (value - high.astype(F32)).astype(BF16)


def spectra_kernel(cycles, noise_ref, refs_ref, trio_ref, cos_ref, sin_ref, bt_ref, hat_ref, swap_ref):
    classes = refs_ref.shape[0] // cycles
    raw = dot(refs_ref[...], trio_ref[...])
    hat = (raw[:, :128] + raw[:, 128:256]) + raw[:, 256:]
    hat_ref[...] = hat
    swap_ref[...] = pltpu.roll(hat, 64, 1)
    cosine, sine = cos_ref[...], sin_ref[...]
    columns = classes * ANGLES

    def body(j, carry):
        weight = noise_ref[j]
        lanes = pl.ds(pl.multiple_of(j * 128, 128), 128)
        for c in range(classes):
            row = pl.ds(c * cycles + j, 1)
            plain = (hat_ref[row, :] * weight).astype(BF16).astype(F32)
            swapped = (swap_ref[row, :] * weight).astype(BF16).astype(F32)
            high, low = halves(plain * cosine + swapped * sine)
            bt_ref[c * ANGLES : (c + 1) * ANGLES, lanes] = high
            bt_ref[columns + c * ANGLES : columns + (c + 1) * ANGLES, lanes] = low
        return carry

    lax.fori_loop(0, cycles, body, 0)


def rotated_spectra(references, inv_noise, cycles):
    classes = references.shape[0]
    refs = references.reshape(classes, 2, cycles, ANGLES).transpose(0, 2, 1, 3)
    refs = refs.reshape(classes * cycles, 2 * ANGLES)
    trio = np.concatenate(split(forward_matrix(), 3), axis=1)
    cosine, sine = rotation_tables()
    vmem = pl.BlockSpec(memory_space=pltpu.VMEM)
    columns = 2 * classes * ANGLES
    return pl.pallas_call(
        functools.partial(spectra_kernel, cycles),
        out_shape=jax.ShapeDtypeStruct((columns, cycles * 128), BF16),
        in_specs=[pl.BlockSpec(memory_space=pltpu.SMEM)] + [vmem] * 4,
        out_specs=vmem,
        scratch_shapes=[pltpu.VMEM((classes * cycles, 128), F32)] * 2,
        compiler_params=pltpu.CompilerParams(vmem_limit_bytes=VMEM_LIMIT),
        cost_estimate=pl.CostEstimate(
            flops=columns * cycles * 128 * 8, bytes_accessed=columns * cycles * 256, transcendentals=0
        ),
        name="rotated_spectra",
    )(inv_noise, refs, jnp.asarray(trio), jnp.asarray(cosine), jnp.asarray(sine))


def bit_reverse(value, bits):
    return sum(((value >> b) & 1) << (bits - 1 - b) for b in range(bits))


def score_kernel(
    cycles,
    slots,
    counts_ref,
    near_ref,
    far_ref,
    offset_ref,
    tc_ref,
    ts_ref,
    forward_ref,
    bt_hbm,
    hat_ref,
    expo_ref,
    stats_ref,
    starts,
    bt_ref,
    plain_ref,
    swap_ref,
    stack_ref,
    sem,
):
    devices = counts_ref.shape[0]
    bits = devices.bit_length() - 1
    me = lax.axis_index("blk")
    chunk = pl.program_id(0)
    copy = pltpu.make_async_copy(bt_hbm, bt_ref, sem)

    @pl.when(chunk == 0)
    def _():
        copy.start()

    def add_start(d, total):
        starts[d] = total
        return total + counts_ref[d]

    lax.fori_loop(0, devices, add_start, jnp.int32(0))

    width = devices // 2 * slots
    lane = lax.broadcasted_iota(jnp.int32, (1, width), 1)
    place = lane % slots
    chosen = None
    for flip, ref in ((0, near_ref), (1, far_ref)):
        rank = jnp.full((1, width), -1, jnp.int32)
        for k in range(devices // 2):
            owner = me ^ (bit_reverse(k, bits) | flip)
            here = (lane // slots == k) & (place < counts_ref[owner])
            rank = jnp.where(here, starts[owner] + place, rank)
        wanted = lax.broadcasted_iota(jnp.int32, (CHUNK, width), 0) + chunk * CHUNK
        pick = (jnp.broadcast_to(rank, (CHUNK, width)) == wanted).astype(F32).astype(BF16)
        term = dot(pick, ref[...])
        chosen = term if chosen is None else chosen + term

    span = cycles * ANGLES
    offset_x = chosen[:, 2 * span : 2 * span + 1]
    offset_y = chosen[:, 2 * span + 1 : 2 * span + 2]
    index = (offset_x + SHIFT // 2) * SHIFT + (offset_y + SHIFT // 2)
    row = lax.broadcasted_iota(jnp.int32, (CHUNK, 96), 1) % 32
    pick = (row.astype(F32) == jnp.broadcast_to(index, (CHUNK, 96))).astype(F32).astype(BF16)
    first = lax.broadcasted_iota(jnp.int32, (CHUNK, 128), 1) < 64
    for jp in range(cycles // 2):
        lanes = slice(jp * 128, jp * 128 + 128)
        cosine = dot(pick, offset_ref[:, lanes])
        sine = dot(pick, offset_ref[:, span + jp * 128 : span + jp * 128 + 128])
        real_in, imag_in = chosen[:, lanes], chosen[:, span + jp * 128 : span + jp * 128 + 128]
        real = real_in * cosine + imag_in * sine
        imag = imag_in * cosine - real_in * sine
        real_roll, imag_roll = pltpu.roll(real, 64, 1), pltpu.roll(imag, 64, 1)
        plain_ref[jp, :, :128] = jnp.where(first, real, imag_roll)
        plain_ref[jp, :, 128:] = jnp.where(first, real_roll, imag)
        swap_ref[jp, :, :128] = jnp.where(first, imag, real_roll)
        swap_ref[jp, :, 128:] = jnp.where(first, imag_roll, real)

    def transform(jp, carry):
        lanes = pl.ds(pl.multiple_of(jp * PAIR, PAIR), PAIR)
        plain, swapped = plain_ref[jp], swap_ref[jp]
        for t in range(STEPS):
            y = plain * tc_ref[t : t + 1, lanes] + swapped * ts_ref[t : t + 1, lanes]
            high, low = halves(y)
            rows = slice(t * CHUNK, (t + 1) * CHUNK)
            stack_ref[0, rows, :128] = high[:, :128]
            stack_ref[0, rows, 128:] = low[:, :128]
            stack_ref[1, rows, :128] = high[:, 128:]
            stack_ref[1, rows, 128:] = low[:, 128:]
        for parity in range(2):
            both = dot(stack_ref[parity], forward_ref[...])
            columns = pl.ds(pl.multiple_of(jp * PAIR + parity * 128, 128), 128)
            hat_ref[0, :, columns] = (both[:, :128] + both[:, 128:]).astype(BF16)
        return carry

    lax.fori_loop(0, cycles // 2, transform, 0)

    @pl.when(chunk == 0)
    def _():
        copy.wait()

    columns = expo_ref.shape[2]
    group = 5 * CHUNK

    def score(i, top):
        rows = pl.ds(pl.multiple_of(i * group, group), group)
        both = dot(hat_ref[0, rows, :], bt_ref[...], ((1,), (1,)))
        scores = both[:, :columns] + both[:, columns:]
        expo_ref[0, rows, :] = scores
        for t in range(5):
            top = jnp.maximum(top, scores[t * CHUNK : (t + 1) * CHUNK])
        return top

    top = lax.fori_loop(0, STEPS // 5, score, jnp.full((CHUNK, columns), -jnp.inf, F32))
    peak = jnp.max(top, axis=1, keepdims=True)

    def exponent(t, total):
        rows = pl.ds(pl.multiple_of(t * CHUNK, CHUNK), CHUNK)
        value = jnp.exp(expo_ref[0, rows, :] - peak)
        expo_ref[0, rows, :] = value
        return total + value

    total = lax.fori_loop(0, STEPS, exponent, jnp.zeros((CHUNK, columns), F32))
    mass = jnp.sum(total, axis=1, keepdims=True)
    diagonal = lax.broadcasted_iota(jnp.int32, (CHUNK, 128), 0) == lax.broadcasted_iota(
        jnp.int32, (CHUNK, 128), 1
    )
    peak_row = jnp.sum(jnp.where(diagonal, peak, 0.0), axis=0, keepdims=True)
    mass_row = jnp.sum(jnp.where(diagonal, mass, 0.0), axis=0, keepdims=True)
    which = lax.broadcasted_iota(jnp.int32, (8, 128), 0)
    tile = jnp.where(which == 0, peak_row, jnp.where(which == 1, mass_row, 0.0))
    stats_ref[...] = jnp.broadcast_to(tile[None, None], stats_ref.shape)


def local_scores(near, far, counts, spectra, cycles, slots, chunks):
    devices = counts.shape[0]
    columns = spectra.shape[0] // 2
    tc, ts = step_tables(cycles)
    whole = lambda shape: pl.BlockSpec(shape, lambda c: (0,) * len(shape))
    table = offset_table(cycles)
    return pl.pallas_call(
        functools.partial(score_kernel, cycles, slots),
        grid=(chunks,),
        out_shape=(
            jax.ShapeDtypeStruct((chunks, ROWS, cycles * 128), BF16),
            jax.ShapeDtypeStruct((chunks, ROWS, columns), F32),
            jax.ShapeDtypeStruct((devices, chunks, 8, 128), F32),
        ),
        in_specs=[
            pl.BlockSpec(memory_space=pltpu.SMEM),
            whole(near.shape),
            whole(far.shape),
            whole(table.shape),
            whole(tc.shape),
            whole(ts.shape),
            whole((256, 256)),
            pl.BlockSpec(memory_space=pl.ANY),
        ],
        out_specs=(
            pl.BlockSpec((1, ROWS, cycles * 128), lambda c: (c, 0, 0)),
            pl.BlockSpec((1, ROWS, columns), lambda c: (c, 0, 0)),
            pl.BlockSpec((devices, 1, 8, 128), lambda c: (0, c, 0, 0)),
        ),
        scratch_shapes=[
            pltpu.SMEM((devices,), jnp.int32),
            pltpu.VMEM(spectra.shape, BF16),
            pltpu.VMEM((cycles // 2, CHUNK, PAIR), F32),
            pltpu.VMEM((cycles // 2, CHUNK, PAIR), F32),
            pltpu.VMEM((2, ROWS, 256), BF16),
            pltpu.SemaphoreType.DMA,
        ],
        compiler_params=pltpu.CompilerParams(vmem_limit_bytes=VMEM_LIMIT),
        name="local_scores",
    )(
        counts,
        near,
        far,
        jnp.asarray(table),
        jnp.asarray(tc),
        jnp.asarray(ts),
        jnp.asarray(forward_stack()),
        spectra,
    )


def sum_kernel(
    classes, counts_ref, stats_ref, expo_ref, hat_ref, cos_ref, sin_ref, image_ref, loglik_ref, out_ref,
    weight_ref, sums_ref,
):
    chunk, jp = pl.program_id(0), pl.program_id(1)
    pairs = pl.num_programs(1)
    me = lax.axis_index("blk")
    columns = classes * ANGLES

    @pl.when(jp == 0)
    def _():
        peaks = stats_ref[:, chunk, 0, :]
        masses = stats_ref[:, chunk, 1, :]
        own_peak = stats_ref[pl.ds(me, 1), chunk, 0, :]
        peak = jnp.max(peaks, axis=0, keepdims=True)
        loglik = peak + jnp.log(jnp.sum(masses * jnp.exp(peaks - peak), axis=0, keepdims=True))
        diagonal = lax.broadcasted_iota(jnp.int32, (CHUNK, 128), 0) == lax.broadcasted_iota(
            jnp.int32, (CHUNK, 128), 1
        )
        column = lambda r: jnp.sum(jnp.where(diagonal, r, 0.0), axis=1, keepdims=True)
        scale = column(jnp.exp(own_peak - loglik))

        def add_start(d, total):
            return total + jnp.where(d < me, counts_ref[d], 0)

        start = lax.fori_loop(0, counts_ref.shape[0], add_start, jnp.int32(0))
        rank = lax.broadcasted_iota(jnp.int32, (CHUNK, 128), 0) + chunk * CHUNK
        slot = lax.broadcasted_iota(jnp.int32, (CHUNK, 128), 1)
        mine = (rank == slot + start) & (slot < counts_ref[me])
        found = jnp.sum(jnp.where(mine, column(loglik), 0.0), axis=0, keepdims=True)

        @pl.when(chunk == 0)
        def _():
            loglik_ref[...] = jnp.zeros_like(loglik_ref)

        loglik_ref[...] += jnp.broadcast_to(found, loglik_ref.shape)

        repeated = jnp.concatenate([scale] * 8, axis=0)

        def weigh(value, width, at):
            high, low = halves(value.T)
            weight_ref[:columns, at : at + width] = high[:, :width]
            weight_ref[columns:, at : at + width] = low[:, :width]

        for block in range(ROWS // 384):
            value = expo_ref[0, block * 384 : (block + 1) * 384, :] * repeated
            for part in range(3):
                weigh(value[part * 128 : (part + 1) * 128], 128, block * 384 + part * 128)
        rest = ROWS % 384
        if rest:
            at = ROWS - rest
            value = expo_ref[0, at:, :] * repeated[:rest]
            value = jnp.concatenate([value, jnp.zeros((128 - rest, columns), F32)], axis=0)
            weigh(value, rest, at)

    both = dot(weight_ref[...], hat_ref[0])
    total = both[:columns] + both[columns:]
    first = lax.broadcasted_iota(jnp.int32, (1, 128), 1) < 64
    height = sums_ref.shape[1]
    rows = []
    for c in range(classes):
        block = total[c * ANGLES : (c + 1) * ANGLES]
        even = jnp.sum(block * cos_ref[...], axis=0, keepdims=True)
        odd = jnp.sum(block * sin_ref[...], axis=0, keepdims=True)
        parts = []
        for parity in range(2):
            lanes = slice(parity * 128, parity * 128 + 128)
            turned = pltpu.roll(odd[:, lanes], 64, 1)
            parts.append(even[:, lanes] + jnp.where(first, -turned, turned))
        rows.append(jnp.concatenate(parts, axis=1))
    if height > classes:
        rows.append(jnp.zeros((height - classes, PAIR), F32))
    value = jnp.concatenate(rows, axis=0)

    @pl.when(chunk == 0)
    def _():
        sums_ref[jp] = value

    @pl.when(chunk > 0)
    def _():
        sums_ref[jp] += value

    @pl.when((chunk == pl.num_programs(0) - 1) & (jp == pairs - 1))
    def _():
        high, low = halves(sums_ref[...].reshape(-1, PAIR))
        upper = dot(high, image_ref[...])
        image = upper[:, :PAIR] + (upper[:, PAIR:] + dot(low, image_ref[:, :PAIR]))
        for q in range(sums_ref.shape[0]):
            for e in range(2):
                out_ref[:, e, q * 128 : (q + 1) * 128] = image[
                    q * height : q * height + classes, e * 128 : (e + 1) * 128
                ]


def local_sums(counts, stats, expo, hat, classes, cycles):
    devices, chunks = stats.shape[:2]
    columns = classes * ANGLES
    pairs = cycles // 2
    cosine, sine = gather_tables()
    whole = lambda shape: pl.BlockSpec(shape, lambda c, j: (0,) * len(shape))
    return pl.pallas_call(
        functools.partial(sum_kernel, classes),
        grid=(chunks, pairs),
        out_shape=(
            jax.ShapeDtypeStruct((8, 128), F32),
            jax.ShapeDtypeStruct((classes, 2, cycles * ANGLES), F32),
        ),
        in_specs=[
            pl.BlockSpec(memory_space=pltpu.SMEM),
            whole(stats.shape),
            pl.BlockSpec((1, ROWS, columns), lambda c, j: (c, 0, 0)),
            pl.BlockSpec((1, ROWS, PAIR), lambda c, j: (c, 0, j)),
            whole((ANGLES, PAIR)),
            whole((ANGLES, PAIR)),
            whole((PAIR, 2 * PAIR)),
        ],
        out_specs=(whole((8, 128)), whole((classes, 2, cycles * ANGLES))),
        scratch_shapes=[
            pltpu.VMEM((2 * columns, ROWS), BF16),
            pltpu.VMEM((pairs, -(-classes // 8) * 8, PAIR), F32),
        ],
        compiler_params=pltpu.CompilerParams(vmem_limit_bytes=VMEM_LIMIT),
        name="local_sums",
    )(counts, stats, expo, hat, jnp.asarray(cosine), jnp.asarray(sine), jnp.asarray(image_stack()))


def local(particles, offsets, references, inv_noise, counts):
    devices = lax.axis_size("blk")
    slots = particles.shape[0]
    cycles = particles.shape[2] // ANGLES
    chunks = MEAN * devices // CHUNK
    classes = references.shape[0]
    spectra = rotated_spectra(references, inv_noise, cycles)
    packed = jnp.concatenate(
        [
            particles.reshape(slots, 2 * cycles * ANGLES),
            jnp.pad(offsets.T.astype(BF16), ((0, 0), (0, 126))),
        ],
        axis=1,
    )
    distance = devices // 2
    while True:
        moved = lax.ppermute(packed, "blk", [(i, i ^ distance) for i in range(devices)])
        if distance == 1:
            break
        packed = jnp.concatenate([packed, moved], axis=0)
        distance //= 2
    hat, expo, stats = local_scores(packed, moved, counts, spectra, cycles, slots, chunks)
    stats = lax.all_to_all(stats, "blk", 0, 0, tiled=True)
    loglik, class_sums = local_sums(counts, stats, expo, hat, classes, cycles)
    return (loglik[0, :slots], class_sums)


def solution(mesh):
    return jax.shard_map(
        local,
        mesh=mesh,
        in_specs=(
            P(("parts", "blk"), None, None),
            P(None, ("parts", "blk")),
            P(("parts", "blk"), None, None),
            P(),
            P("parts"),
        ),
        out_specs=(P(("parts", "blk")), P(("parts", "blk"), None, None)),
        check_vma=False,
    )
```

```python
import functools
import math

import jax
import jax.numpy as jnp
import numpy as np
from jax import lax
from jax.experimental import pallas as pl
from jax.experimental.pallas import tpu as pltpu
from jax.sharding import PartitionSpec as P

ANGLES = 64
SHIFT = 5
STEPS = SHIFT * SHIFT
MEAN = 3
CHUNK = 48
ROWS = STEPS * CHUNK
PAIR = 4 * ANGLES
WIDE = 16
STEP_GROUPS = tuple(tuple(g) for g in (range(i, min(i + 9, STEPS)) for i in range(0, STEPS, 9)))
F32 = jnp.float32
BF16 = jnp.bfloat16
MIB = 1024 * 1024


def split(table, terms):
    rest = np.asarray(table, np.float64)
    out = []
    for _ in range(terms):
        piece = rest.astype(np.float32).astype(jnp.bfloat16)
        out.append(piece)
        rest = rest - piece.astype(np.float64)
    return out


def angle_products():
    index = np.arange(ANGLES)
    radians = 2.0 * math.pi / ANGLES * (index[:, None] * index[None, :] % ANGLES)
    return np.cos(radians), np.sin(radians)


def step_phases(cycles):
    polar = 2.0 * math.pi / ANGLES * np.arange(ANGLES)
    radius = np.arange(1, cycles + 1)
    step = np.arange(STEPS)
    along = (step // SHIFT - SHIFT // 2)[:, None] * np.cos(polar) + (step % SHIFT - SHIFT // 2)[
        :, None
    ] * np.sin(polar)
    phases = 2.0 * math.pi / 128.0 * radius[None, :, None] * along[:, None, :]
    return np.cos(phases), np.sin(phases)


def step_tables(cycles):
    cosine, sine = step_phases(cycles)
    tc = np.concatenate([cosine, cosine], axis=2).reshape(STEPS, -1).astype(np.float32)
    ts = np.concatenate([sine, -sine], axis=2).reshape(STEPS, -1).astype(np.float32)
    return tc, ts


def offset_table(cycles):
    cosine, sine = step_phases(cycles)
    both = np.concatenate([cosine.reshape(STEPS, -1), sine.reshape(STEPS, -1)], axis=1)
    both = np.pad(both, ((0, 32 - STEPS), (0, 0)))
    return np.concatenate(split(both, 3), axis=0)


def forward_matrix():
    cosine, sine = angle_products()
    return np.block([[cosine, -sine], [sine, cosine]])


def forward_stack():
    high, low = split(forward_matrix(), 2)
    return np.block([[high, low], [high, np.zeros_like(low)]])


def rotation_tables():
    cosine, sine = angle_products()
    cosine, sine = cosine / ANGLES, sine / ANGLES
    return (
        np.concatenate([cosine, cosine], axis=1).astype(np.float32),
        np.concatenate([sine, -sine], axis=1).astype(np.float32),
    )


def gather_tables():
    cosine, sine = angle_products()
    return (
        np.concatenate([cosine] * 4, axis=1).astype(np.float32),
        np.concatenate([sine] * 4, axis=1).astype(np.float32),
    )


def image_stack():
    cosine, sine = angle_products()
    table = np.zeros((2, 2, ANGLES, 2, 2, ANGLES))
    for parity in range(2):
        table[parity, 0, :, 0, parity] = cosine / ANGLES
        table[parity, 1, :, 0, parity] = -sine / ANGLES
        table[parity, 0, :, 1, parity] = sine / ANGLES
        table[parity, 1, :, 1, parity] = cosine / ANGLES
    high, low = split(table.reshape(PAIR, PAIR), 2)
    return np.concatenate([high, low], axis=1)


def dot(left, right, dims=((1,), (0,))):
    return lax.dot_general(left, right, (dims, ((), ())), preferred_element_type=F32)


def halves(value):
    high = value.astype(BF16)
    return high, (value - high.astype(F32)).astype(BF16)


def spectra_kernel(cycles, noise_ref, refs_ref, trio_ref, cos_ref, sin_ref, bt_ref, hat_ref, swap_ref):
    classes = refs_ref.shape[0] // cycles
    raw = dot(refs_ref[...], trio_ref[...])
    hat = (raw[:, :128] + raw[:, 128:256]) + raw[:, 256:]
    hat_ref[...] = hat
    swap_ref[...] = pltpu.roll(hat, 64, 1)
    cosine, sine = cos_ref[...], sin_ref[...]
    columns = classes * ANGLES

    def body(j, carry):
        weight = noise_ref[j]
        lanes = pl.ds(pl.multiple_of(j * 128, 128), 128)
        for c in range(classes):
            row = pl.ds(c * cycles + j, 1)
            plain = (hat_ref[row, :] * weight).astype(BF16).astype(F32)
            swapped = (swap_ref[row, :] * weight).astype(BF16).astype(F32)
            high, low = halves(plain * cosine + swapped * sine)
            bt_ref[c * ANGLES : (c + 1) * ANGLES, lanes] = high
            bt_ref[columns + c * ANGLES : columns + (c + 1) * ANGLES, lanes] = low
        return carry

    lax.fori_loop(0, cycles, body, 0)


def rotated_spectra(references, inv_noise, cycles):
    classes = references.shape[0]
    refs = references.reshape(classes, 2, cycles, ANGLES).transpose(0, 2, 1, 3)
    refs = refs.reshape(classes * cycles, 2 * ANGLES)
    trio = np.concatenate(split(forward_matrix(), 3), axis=1)
    cosine, sine = rotation_tables()
    vmem = pl.BlockSpec(memory_space=pltpu.VMEM)
    columns = 2 * classes * ANGLES
    return pl.pallas_call(
        functools.partial(spectra_kernel, cycles),
        out_shape=pltpu.VMEM((columns, cycles * 128), BF16),
        in_specs=[pl.BlockSpec(memory_space=pltpu.SMEM)] + [vmem] * 4,
        out_specs=vmem,
        scratch_shapes=[pltpu.VMEM((classes * cycles, 128), F32)] * 2,
        compiler_params=pltpu.CompilerParams(vmem_limit_bytes=16 * MIB),
        cost_estimate=pl.CostEstimate(
            flops=columns * cycles * 128 * 8, bytes_accessed=columns * cycles * 256, transcendentals=0
        ),
        name="rotated_spectra",
    )(inv_noise, refs, jnp.asarray(trio), jnp.asarray(cosine), jnp.asarray(sine))


def bit_reverse(value, bits):
    return sum(((value >> b) & 1) << (bits - 1 - b) for b in range(bits))


def pack_kernel(particles_hbm, offsets_hbm, out_ref, particles_ref, offsets_ref, sems):
    slots, span = particles_ref.shape[0], particles_ref.shape[2]
    copies = [
        pltpu.make_async_copy(particles_hbm, particles_ref, sems.at[0]),
        pltpu.make_async_copy(offsets_hbm, offsets_ref, sems.at[1]),
    ]
    for copy in copies:
        copy.start()
    for copy in copies:
        copy.wait()
    values = particles_ref[...].astype(F32)
    out_ref[:, :span] = values[:, 0, :].astype(BF16)
    out_ref[:, span : 2 * span] = values[:, 1, :].astype(BF16)
    offsets = offsets_ref[...].astype(F32)
    diagonal = lax.broadcasted_iota(jnp.int32, (slots, slots), 0) == lax.broadcasted_iota(
        jnp.int32, (slots, slots), 1
    )
    lane = lax.broadcasted_iota(jnp.int32, (slots, 128), 1)
    tail = jnp.zeros((slots, 128), F32)
    for axis in range(2):
        column = jnp.sum(jnp.where(diagonal, offsets[axis : axis + 1], 0.0), axis=1, keepdims=True)
        tail = jnp.where(lane == axis, column, tail)
    out_ref[:, 2 * span :] = tail.astype(BF16)


def pack(particles, offsets):
    slots, _, span = particles.shape
    vmem = pl.BlockSpec(memory_space=pltpu.VMEM)
    return pl.pallas_call(
        pack_kernel,
        out_shape=pltpu.VMEM((slots, 2 * span + 128), BF16),
        in_specs=[pl.BlockSpec(memory_space=pltpu.HBM)] * 2,
        out_specs=vmem,
        scratch_shapes=[
            pltpu.VMEM(particles.shape, particles.dtype),
            pltpu.VMEM(offsets.shape, offsets.dtype),
            pltpu.SemaphoreType.DMA((2,)),
        ],
        compiler_params=pltpu.CompilerParams(vmem_limit_bytes=2 * 1024 * 1024),
        name="pack",
    )(
        pltpu.with_memory_space_constraint(particles, pltpu.HBM),
        pltpu.with_memory_space_constraint(offsets, pltpu.HBM),
    )


def find_starts(counts_ref, starts):
    def add_start(d, total):
        starts[d] = total
        return total + counts_ref[d]

    lax.fori_loop(0, counts_ref.shape[0], add_start, jnp.int32(0))


def score_chunk(
    cycles, slots, chunk, counts_ref, near_ref, far_ref, offset_ref, tc_ref, ts_ref, forward_ref, bt_ref,
    hat_ref, expo_ref, stats_ref, starts, plain_ref, swap_ref, stack_ref,
):
    devices = counts_ref.shape[0]
    bits = devices.bit_length() - 1
    me = lax.axis_index("blk")
    width = devices // 2 * slots
    lane = lax.broadcasted_iota(jnp.int32, (1, width), 1)
    place = lane % slots
    chosen = None
    for flip, ref in ((0, near_ref), (1, far_ref)):
        rank = jnp.full((1, width), -1, jnp.int32)
        for k in range(devices // 2):
            owner = me ^ (bit_reverse(k, bits) | flip)
            here = (lane // slots == k) & (place < counts_ref[owner])
            rank = jnp.where(here, starts[owner] + place, rank)
        wanted = lax.broadcasted_iota(jnp.int32, (CHUNK, width), 0) + chunk * CHUNK
        pick = (jnp.broadcast_to(rank, (CHUNK, width)) == wanted).astype(F32).astype(BF16)
        term = dot(pick, ref[...])
        chosen = term if chosen is None else chosen + term

    span = cycles * ANGLES
    offset_x = chosen[:, 2 * span : 2 * span + 1]
    offset_y = chosen[:, 2 * span + 1 : 2 * span + 2]
    index = (offset_x + SHIFT // 2) * SHIFT + (offset_y + SHIFT // 2)
    row = lax.broadcasted_iota(jnp.int32, (CHUNK, 96), 1) % 32
    pick = (row.astype(F32) == jnp.broadcast_to(index, (CHUNK, 96))).astype(F32).astype(BF16)
    first = lax.broadcasted_iota(jnp.int32, (CHUNK, 128), 1) < 64
    for jp in range(cycles // 2):
        lanes = slice(jp * 128, jp * 128 + 128)
        cosine = dot(pick, offset_ref[:, lanes])
        sine = dot(pick, offset_ref[:, span + jp * 128 : span + jp * 128 + 128])
        real_in, imag_in = chosen[:, lanes], chosen[:, span + jp * 128 : span + jp * 128 + 128]
        real = real_in * cosine + imag_in * sine
        imag = imag_in * cosine - real_in * sine
        real_roll, imag_roll = pltpu.roll(real, 64, 1), pltpu.roll(imag, 64, 1)
        plain_ref[jp, :, :128] = jnp.where(first, real, imag_roll)
        plain_ref[jp, :, 128:] = jnp.where(first, real_roll, imag)
        swap_ref[jp, :, :128] = jnp.where(first, imag, real_roll)
        swap_ref[jp, :, 128:] = jnp.where(first, imag_roll, real)

    def transform(jp, carry):
        lanes = pl.ds(pl.multiple_of(jp * PAIR, PAIR), PAIR)
        plain, swapped = plain_ref[jp], swap_ref[jp]
        for steps in STEP_GROUPS:
            for t in steps:
                y = plain * tc_ref[t : t + 1, lanes] + swapped * ts_ref[t : t + 1, lanes]
                high, low = halves(y)
                rows = slice(t * CHUNK, (t + 1) * CHUNK)
                stack_ref[0, rows, :128] = high[:, :128]
                stack_ref[0, rows, 128:] = low[:, :128]
                stack_ref[1, rows, :128] = high[:, 128:]
                stack_ref[1, rows, 128:] = low[:, 128:]
            rows = slice(steps[0] * CHUNK, (steps[-1] + 1) * CHUNK)
            for parity in range(2):
                both = dot(stack_ref[parity, rows], forward_ref[...])
                columns = pl.ds(pl.multiple_of(jp * PAIR + parity * 128, 128), 128)
                hat_ref[rows, columns] = (both[:, :128] + both[:, 128:]).astype(BF16)
        return carry

    lax.fori_loop(0, cycles // 2, transform, 0)

    columns = expo_ref.shape[1]
    both = dot(hat_ref[...], bt_ref[...], ((1,), (1,)))
    expo_ref[...] = both[:, :columns] + both[:, columns:]
    step_rows = [slice(t * CHUNK, (t + 1) * CHUNK) for t in range(STEPS)]
    top = expo_ref[step_rows[0], :]
    for rows in step_rows[1:]:
        top = jnp.maximum(top, expo_ref[rows, :])
    peak = jnp.max(top, axis=1, keepdims=True)
    total = jnp.zeros((CHUNK, columns), F32)
    for rows in step_rows:
        value = jnp.exp(expo_ref[rows, :] - peak)
        expo_ref[rows, :] = value
        total = total + value
    mass = jnp.sum(total, axis=1, keepdims=True)
    diagonal = lax.broadcasted_iota(jnp.int32, (CHUNK, 128), 0) == lax.broadcasted_iota(
        jnp.int32, (CHUNK, 128), 1
    )
    peak_row = jnp.sum(jnp.where(diagonal, peak, 0.0), axis=0, keepdims=True)
    mass_row = jnp.sum(jnp.where(diagonal, mass, 0.0), axis=0, keepdims=True)
    which = lax.broadcasted_iota(jnp.int32, (8, 128), 0)
    tile = jnp.where(which == 0, peak_row, jnp.where(which == 1, mass_row, 0.0))
    for d in range(devices):
        stats_ref[d, chunk] = tile


def score_kernel(
    cycles, slots, chunks, counts_ref, near_ref, far_ref, offset_ref, tc_ref, ts_ref, forward_ref, bt_ref,
    hat_ref, expo_ref, stats_ref, starts, plain_ref, swap_ref, stack_ref, *spare,
):
    find_starts(counts_ref, starts)
    given = (counts_ref, near_ref, far_ref, offset_ref, tc_ref, ts_ref, forward_ref, bt_ref)
    held = (stats_ref, starts, plain_ref, swap_ref, stack_ref)
    if chunks == 1:
        score_chunk(cycles, slots, 0, *given, hat_ref, expo_ref, *held)
        return
    hat_now, expo_now = spare

    def body(chunk, carry):
        score_chunk(cycles, slots, chunk, *given, hat_now, expo_now, *held)
        pltpu.sync_copy(hat_now, hat_ref.at[chunk])
        pltpu.sync_copy(expo_now, expo_ref.at[chunk])
        return carry

    lax.fori_loop(0, chunks, body, 0)


def local_scores(near, far, counts, spectra, cycles, slots, chunks):
    devices = counts.shape[0]
    columns = spectra.shape[0] // 2
    tc, ts = step_tables(cycles)
    table = offset_table(cycles)
    vmem = pl.BlockSpec(memory_space=pltpu.VMEM)
    hat, expo = (ROWS, cycles * 128), (ROWS, columns)
    if chunks == 1:
        kept = (pltpu.VMEM(hat, BF16), pltpu.VMEM(expo, F32))
        place, spare = vmem, []
    else:
        kept = (
            jax.ShapeDtypeStruct((chunks, *hat), BF16),
            jax.ShapeDtypeStruct((chunks, *expo), F32),
        )
        place, spare = pl.BlockSpec(memory_space=pl.ANY), [pltpu.VMEM(hat, BF16), pltpu.VMEM(expo, F32)]
    return pl.pallas_call(
        functools.partial(score_kernel, cycles, slots, chunks),
        out_shape=(*kept, jax.ShapeDtypeStruct((devices, chunks, 8, 128), F32)),
        in_specs=[pl.BlockSpec(memory_space=pltpu.SMEM)] + [vmem] * 7,
        out_specs=(place, place, vmem),
        scratch_shapes=[
            pltpu.SMEM((devices,), jnp.int32),
            pltpu.VMEM((cycles // 2, CHUNK, PAIR), F32),
            pltpu.VMEM((cycles // 2, CHUNK, PAIR), F32),
            pltpu.VMEM((2, ROWS, 256), BF16),
            *spare,
        ],
        compiler_params=pltpu.CompilerParams(vmem_limit_bytes=(16 if chunks == 1 else 40) * MIB),
        name="local_scores",
    )(
        counts, near, far, jnp.asarray(table), jnp.asarray(tc), jnp.asarray(ts), jnp.asarray(forward_stack()),
        pltpu.with_memory_space_constraint(spectra, pltpu.VMEM),
    )


def sum_chunk(
    classes, chunk, counts_ref, stats_ref, expo_ref, hat_ref, cos_ref, sin_ref, loglik_ref, weight_ref, sums_ref,
):
    slots = loglik_ref.shape[1]
    me = lax.axis_index("blk")
    columns = classes * ANGLES
    peaks = stats_ref[:, chunk, 0, :]
    masses = stats_ref[:, chunk, 1, :]
    own_peak = stats_ref[pl.ds(me, 1), chunk, 0, :]
    peak = jnp.max(peaks, axis=0, keepdims=True)
    loglik = peak + jnp.log(jnp.sum(masses * jnp.exp(peaks - peak), axis=0, keepdims=True))
    diagonal = lax.broadcasted_iota(jnp.int32, (CHUNK, 128), 0) == lax.broadcasted_iota(
        jnp.int32, (CHUNK, 128), 1
    )
    column = lambda r: jnp.sum(jnp.where(diagonal, r, 0.0), axis=1, keepdims=True)
    scale = column(jnp.exp(own_peak - loglik))

    def add_start(d, total):
        return total + jnp.where(d < me, counts_ref[d], 0)

    start = lax.fori_loop(0, counts_ref.shape[0], add_start, jnp.int32(0))
    rank = lax.broadcasted_iota(jnp.int32, (CHUNK, slots), 0) + chunk * CHUNK
    slot = lax.broadcasted_iota(jnp.int32, (CHUNK, slots), 1)
    mine = (rank == slot + start) & (slot < counts_ref[me])
    loglik_ref[...] += jnp.sum(jnp.where(mine, column(loglik), 0.0), axis=0, keepdims=True)

    repeated = jnp.concatenate([scale] * 8, axis=0)

    def weigh(value, width, at):
        high, low = halves(value.T)
        weight_ref[:columns, at : at + width] = high[:, :width]
        weight_ref[columns:, at : at + width] = low[:, :width]

    for block in range(ROWS // 384):
        value = expo_ref[block * 384 : (block + 1) * 384, :] * repeated
        for part in range(3):
            weigh(value[part * 128 : (part + 1) * 128], 128, block * 384 + part * 128)
    rest = ROWS % 384
    if rest:
        at = ROWS - rest
        value = expo_ref[at:, :] * repeated[:rest]
        value = jnp.concatenate([value, jnp.zeros((128 - rest, columns), F32)], axis=0)
        weigh(value, rest, at)

    first = lax.broadcasted_iota(jnp.int32, (1, 128), 1) < 64
    height = sums_ref.shape[1]

    def body(i, carry):
        lanes = pl.ds(pl.multiple_of(i * (WIDE * PAIR), WIDE * PAIR), WIDE * PAIR)
        both = dot(weight_ref[...], hat_ref[:, lanes])
        totals = both[:columns] + both[columns:]
        for q in range(WIDE):
            turn_back(i * WIDE + q, totals[:, q * PAIR : (q + 1) * PAIR])
        return carry

    def turn_back(jp, total):
        rows = []
        for c in range(classes):
            block = total[c * ANGLES : (c + 1) * ANGLES]
            even = jnp.sum(block * cos_ref[...], axis=0, keepdims=True)
            odd = jnp.sum(block * sin_ref[...], axis=0, keepdims=True)
            parts = []
            for parity in range(2):
                part = slice(parity * 128, parity * 128 + 128)
                turned = pltpu.roll(odd[:, part], 64, 1)
                parts.append(even[:, part] + jnp.where(first, -turned, turned))
            rows.append(jnp.concatenate(parts, axis=1))
        if height > classes:
            rows.append(jnp.zeros((height - classes, PAIR), F32))
        sums_ref[jp] += jnp.concatenate(rows, axis=0)

    lax.fori_loop(0, sums_ref.shape[0] // WIDE, body, 0)


def sum_kernel(
    classes, chunks, counts_ref, stats_ref, expo_ref, hat_ref, cos_ref, sin_ref, image_ref, loglik_ref, out_ref,
    weight_ref, sums_ref, *spare,
):
    loglik_ref[...] = jnp.zeros_like(loglik_ref)
    sums_ref[...] = jnp.zeros_like(sums_ref)
    tables = (cos_ref, sin_ref, loglik_ref, weight_ref, sums_ref)
    if chunks == 1:
        sum_chunk(classes, 0, counts_ref, stats_ref, expo_ref, hat_ref, *tables)
    else:
        hat_now, expo_now = spare

        def body(chunk, carry):
            pltpu.sync_copy(hat_ref.at[chunk], hat_now)
            pltpu.sync_copy(expo_ref.at[chunk], expo_now)
            sum_chunk(classes, chunk, counts_ref, stats_ref, expo_now, hat_now, *tables)
            return carry

        lax.fori_loop(0, chunks, body, 0)

    height = sums_ref.shape[1]
    high, low = halves(sums_ref[...].reshape(-1, PAIR))
    upper = dot(high, image_ref[...])
    image = upper[:, :PAIR] + (upper[:, PAIR:] + dot(low, image_ref[:, :PAIR]))
    for q in range(sums_ref.shape[0]):
        for e in range(2):
            out_ref[:, e, q * 128 : (q + 1) * 128] = image[
                q * height : q * height + classes, e * 128 : (e + 1) * 128
            ]


def local_sums(counts, stats, expo, hat, classes, cycles, slots, chunks):
    columns = classes * ANGLES
    pairs = cycles // 2
    cosine, sine = gather_tables()
    vmem = pl.BlockSpec(memory_space=pltpu.VMEM)
    place, spare = vmem, []
    if chunks > 1:
        place = pl.BlockSpec(memory_space=pl.ANY)
        spare = [pltpu.VMEM((ROWS, cycles * 128), BF16), pltpu.VMEM((ROWS, columns), F32)]
    return pl.pallas_call(
        functools.partial(sum_kernel, classes, chunks),
        out_shape=(
            jax.ShapeDtypeStruct((1, slots), F32),
            jax.ShapeDtypeStruct((classes, 2, cycles * ANGLES), F32),
        ),
        in_specs=[pl.BlockSpec(memory_space=pltpu.SMEM), vmem, place, place, vmem, vmem, vmem],
        out_specs=(vmem, vmem),
        scratch_shapes=[
            pltpu.VMEM((2 * columns, ROWS), BF16),
            pltpu.VMEM((pairs, -(-classes // 8) * 8, PAIR), F32),
            *spare,
        ],
        compiler_params=pltpu.CompilerParams(vmem_limit_bytes=(16 if chunks == 1 else 40) * MIB),
        name="local_sums",
    )(counts, stats, expo, hat, jnp.asarray(cosine), jnp.asarray(sine), jnp.asarray(image_stack()))


def local(particles, offsets, references, inv_noise, counts):
    devices = lax.axis_size("blk")
    slots = particles.shape[0]
    cycles = particles.shape[2] // ANGLES
    chunks = MEAN * devices // CHUNK
    classes = references.shape[0]
    packed = pack(particles, offsets)
    distance = devices // 2
    while True:
        if distance == 2:
            moved = lax.ppermute(packed, "blk", [(i, i ^ distance) for i in range(devices)])
            spectra = rotated_spectra(references, inv_noise, cycles)
            moved, spectra = lax.optimization_barrier((moved, spectra))
        else:
            moved = lax.ppermute(packed, "blk", [(i, i ^ distance) for i in range(devices)])
        if distance == 1:
            break
        packed = jnp.concatenate([packed, moved], axis=0)
        distance //= 2
    hat, expo, stats = local_scores(packed, moved, counts, spectra, cycles, slots, chunks)
    stats = lax.all_to_all(stats, "blk", 0, 0, tiled=True)
    loglik, class_sums = local_sums(counts, stats, expo, hat, classes, cycles, slots, chunks)
    return (loglik.reshape(slots), class_sums)


def solution(mesh):
    return jax.shard_map(
        local,
        mesh=mesh,
        in_specs=(
            P(("parts", "blk"), None, None),
            P(None, ("parts", "blk")),
            P(("parts", "blk"), None, None),
            P(),
            P("parts"),
        ),
        out_specs=(P(("parts", "blk")), P(("parts", "blk"), None, None)),
        check_vma=False,
    )
```

```python
import functools
import math

import jax
import jax.numpy as jnp
import numpy as np
from jax import lax
from jax.experimental import pallas as pl
from jax.experimental.pallas import tpu as pltpu
from jax.sharding import PartitionSpec as P

ANGLES = 64
SHIFT = 5
STEPS = SHIFT * SHIFT
MEAN = 3
CHUNK = 48
ROWS = STEPS * CHUNK
PAIR = 4 * ANGLES
WIDE = 16
STEP_GROUPS = tuple(tuple(g) for g in (range(i, min(i + 9, STEPS)) for i in range(0, STEPS, 9)))
F32 = jnp.float32
BF16 = jnp.bfloat16
MIB = 1024 * 1024


def split(table, terms):
    rest = np.asarray(table, np.float64)
    out = []
    for _ in range(terms):
        piece = rest.astype(np.float32).astype(jnp.bfloat16)
        out.append(piece)
        rest = rest - piece.astype(np.float64)
    return out


def angle_products():
    index = np.arange(ANGLES)
    radians = 2.0 * math.pi / ANGLES * (index[:, None] * index[None, :] % ANGLES)
    return np.cos(radians), np.sin(radians)


def step_phases(cycles):
    polar = 2.0 * math.pi / ANGLES * np.arange(ANGLES)
    radius = np.arange(1, cycles + 1)
    step = np.arange(STEPS)
    along = (step // SHIFT - SHIFT // 2)[:, None] * np.cos(polar) + (step % SHIFT - SHIFT // 2)[
        :, None
    ] * np.sin(polar)
    phases = 2.0 * math.pi / 128.0 * radius[None, :, None] * along[:, None, :]
    return np.cos(phases), np.sin(phases)


def step_tables(cycles):
    cosine, sine = step_phases(cycles)
    tc = np.concatenate([cosine, cosine], axis=2).reshape(STEPS, -1).astype(np.float32)
    ts = np.concatenate([sine, -sine], axis=2).reshape(STEPS, -1).astype(np.float32)
    return tc, ts


def offset_table(cycles):
    cosine, sine = step_phases(cycles)
    both = np.concatenate([cosine.reshape(STEPS, -1), sine.reshape(STEPS, -1)], axis=1)
    both = np.pad(both, ((0, 32 - STEPS), (0, 0)))
    return np.concatenate(split(both, 3), axis=0)


def forward_matrix():
    cosine, sine = angle_products()
    return np.block([[cosine, -sine], [sine, cosine]])


def forward_stack():
    high, low = split(forward_matrix(), 2)
    return np.block([[high, low], [high, np.zeros_like(low)]])


def rotation_tables():
    cosine, sine = angle_products()
    cosine, sine = cosine / ANGLES, sine / ANGLES
    return (
        np.concatenate([cosine, cosine], axis=1).astype(np.float32),
        np.concatenate([sine, -sine], axis=1).astype(np.float32),
    )


def gather_tables():
    cosine, sine = angle_products()
    return (
        np.concatenate([cosine] * 4, axis=1).astype(np.float32),
        np.concatenate([sine] * 4, axis=1).astype(np.float32),
    )


def image_stack():
    cosine, sine = angle_products()
    table = np.zeros((2, 2, ANGLES, 2, 2, ANGLES))
    for parity in range(2):
        table[parity, 0, :, 0, parity] = cosine / ANGLES
        table[parity, 1, :, 0, parity] = -sine / ANGLES
        table[parity, 0, :, 1, parity] = sine / ANGLES
        table[parity, 1, :, 1, parity] = cosine / ANGLES
    high, low = split(table.reshape(PAIR, PAIR), 2)
    return np.concatenate([high, low], axis=1)


def dot(left, right, dims=((1,), (0,))):
    return lax.dot_general(left, right, (dims, ((), ())), preferred_element_type=F32)


def halves(value):
    high = value.astype(BF16)
    return high, (value - high.astype(F32)).astype(BF16)


def spectra_kernel(cycles, noise_ref, refs_ref, trio_ref, cos_ref, sin_ref, bt_ref, hat_ref, swap_ref):
    classes = refs_ref.shape[0] // cycles
    raw = dot(refs_ref[...], trio_ref[...])
    hat = (raw[:, :128] + raw[:, 128:256]) + raw[:, 256:]
    hat_ref[...] = hat
    swap_ref[...] = pltpu.roll(hat, 64, 1)
    cosine, sine = cos_ref[...], sin_ref[...]
    columns = classes * ANGLES

    def body(j, carry):
        weight = noise_ref[j]
        lanes = pl.ds(pl.multiple_of(j * 128, 128), 128)
        for c in range(classes):
            row = pl.ds(c * cycles + j, 1)
            plain = (hat_ref[row, :] * weight).astype(BF16).astype(F32)
            swapped = (swap_ref[row, :] * weight).astype(BF16).astype(F32)
            high, low = halves(plain * cosine + swapped * sine)
            bt_ref[c * ANGLES : (c + 1) * ANGLES, lanes] = high
            bt_ref[columns + c * ANGLES : columns + (c + 1) * ANGLES, lanes] = low
        return carry

    lax.fori_loop(0, cycles, body, 0)


def rotated_spectra(references, inv_noise, cycles):
    classes = references.shape[0]
    refs = references.reshape(classes, 2, cycles, ANGLES).transpose(0, 2, 1, 3)
    refs = refs.reshape(classes * cycles, 2 * ANGLES)
    trio = np.concatenate(split(forward_matrix(), 3), axis=1)
    cosine, sine = rotation_tables()
    vmem = pl.BlockSpec(memory_space=pltpu.VMEM)
    columns = 2 * classes * ANGLES
    return pl.pallas_call(
        functools.partial(spectra_kernel, cycles),
        out_shape=pltpu.VMEM((columns, cycles * 128), BF16),
        in_specs=[pl.BlockSpec(memory_space=pltpu.SMEM)] + [vmem] * 4,
        out_specs=vmem,
        scratch_shapes=[pltpu.VMEM((classes * cycles, 128), F32)] * 2,
        compiler_params=pltpu.CompilerParams(vmem_limit_bytes=16 * MIB),
        cost_estimate=pl.CostEstimate(
            flops=columns * cycles * 128 * 8, bytes_accessed=columns * cycles * 256, transcendentals=0
        ),
        name="rotated_spectra",
    )(inv_noise, refs, jnp.asarray(trio), jnp.asarray(cosine), jnp.asarray(sine))


def bit_reverse(value, bits):
    return sum(((value >> b) & 1) << (bits - 1 - b) for b in range(bits))


def pack_kernel(particles_hbm, offsets_hbm, out_ref, particles_ref, offsets_ref, sems):
    slots, span = particles_ref.shape[0], particles_ref.shape[2]
    copies = [
        pltpu.make_async_copy(particles_hbm, particles_ref, sems.at[0]),
        pltpu.make_async_copy(offsets_hbm, offsets_ref, sems.at[1]),
    ]
    for copy in copies:
        copy.start()
    for copy in copies:
        copy.wait()
    values = particles_ref[...].astype(F32)
    out_ref[:, :span] = values[:, 0, :].astype(BF16)
    out_ref[:, span : 2 * span] = values[:, 1, :].astype(BF16)
    offsets = offsets_ref[...].astype(F32)
    diagonal = lax.broadcasted_iota(jnp.int32, (slots, slots), 0) == lax.broadcasted_iota(
        jnp.int32, (slots, slots), 1
    )
    lane = lax.broadcasted_iota(jnp.int32, (slots, 128), 1)
    tail = jnp.zeros((slots, 128), F32)
    for axis in range(2):
        column = jnp.sum(jnp.where(diagonal, offsets[axis : axis + 1], 0.0), axis=1, keepdims=True)
        tail = jnp.where(lane == axis, column, tail)
    out_ref[:, 2 * span :] = tail.astype(BF16)


def pack(particles, offsets):
    slots, _, span = particles.shape
    vmem = pl.BlockSpec(memory_space=pltpu.VMEM)
    return pl.pallas_call(
        pack_kernel,
        out_shape=pltpu.VMEM((slots, 2 * span + 128), BF16),
        in_specs=[pl.BlockSpec(memory_space=pltpu.HBM)] * 2,
        out_specs=vmem,
        scratch_shapes=[
            pltpu.VMEM(particles.shape, particles.dtype),
            pltpu.VMEM(offsets.shape, offsets.dtype),
            pltpu.SemaphoreType.DMA((2,)),
        ],
        compiler_params=pltpu.CompilerParams(vmem_limit_bytes=2 * 1024 * 1024),
        name="pack",
    )(
        pltpu.with_memory_space_constraint(particles, pltpu.HBM),
        pltpu.with_memory_space_constraint(offsets, pltpu.HBM),
    )


def find_starts(counts_ref, starts):
    def add_start(d, total):
        starts[d] = total
        return total + counts_ref[d]

    lax.fori_loop(0, counts_ref.shape[0], add_start, jnp.int32(0))


def score_chunk(
    cycles, slots, chunk, counts_ref, near_ref, far_ref, offset_ref, tc_ref, ts_ref, forward_ref, bt_ref,
    hat_ref, expo_ref, stats_ref, starts, plain_ref, swap_ref, stack_ref,
):
    devices = counts_ref.shape[0]
    bits = devices.bit_length() - 1
    me = lax.axis_index("blk")
    width = devices // 2 * slots
    lane = lax.broadcasted_iota(jnp.int32, (1, width), 1)
    place = lane % slots
    chosen = None
    for flip, ref in ((0, near_ref), (1, far_ref)):
        rank = jnp.full((1, width), -1, jnp.int32)
        for k in range(devices // 2):
            owner = me ^ (bit_reverse(k, bits) | flip)
            here = (lane // slots == k) & (place < counts_ref[owner])
            rank = jnp.where(here, starts[owner] + place, rank)
        wanted = lax.broadcasted_iota(jnp.int32, (CHUNK, width), 0) + chunk * CHUNK
        pick = (jnp.broadcast_to(rank, (CHUNK, width)) == wanted).astype(F32).astype(BF16)
        term = dot(pick, ref[...])
        chosen = term if chosen is None else chosen + term

    span = cycles * ANGLES
    offset_x = chosen[:, 2 * span : 2 * span + 1]
    offset_y = chosen[:, 2 * span + 1 : 2 * span + 2]
    index = (offset_x + SHIFT // 2) * SHIFT + (offset_y + SHIFT // 2)
    row = lax.broadcasted_iota(jnp.int32, (CHUNK, 96), 1) % 32
    pick = (row.astype(F32) == jnp.broadcast_to(index, (CHUNK, 96))).astype(F32).astype(BF16)
    first = lax.broadcasted_iota(jnp.int32, (CHUNK, 128), 1) < 64
    for jp in range(cycles // 2):
        lanes = slice(jp * 128, jp * 128 + 128)
        cosine = dot(pick, offset_ref[:, lanes])
        sine = dot(pick, offset_ref[:, span + jp * 128 : span + jp * 128 + 128])
        real_in, imag_in = chosen[:, lanes], chosen[:, span + jp * 128 : span + jp * 128 + 128]
        real = real_in * cosine + imag_in * sine
        imag = imag_in * cosine - real_in * sine
        real_roll, imag_roll = pltpu.roll(real, 64, 1), pltpu.roll(imag, 64, 1)
        plain_ref[jp, :, :128] = jnp.where(first, real, imag_roll)
        plain_ref[jp, :, 128:] = jnp.where(first, real_roll, imag)
        swap_ref[jp, :, :128] = jnp.where(first, imag, real_roll)
        swap_ref[jp, :, 128:] = jnp.where(first, imag_roll, real)

    def transform(jp, carry):
        lanes = pl.ds(pl.multiple_of(jp * PAIR, PAIR), PAIR)
        plain, swapped = plain_ref[jp], swap_ref[jp]
        for steps in STEP_GROUPS:
            for t in steps:
                y = plain * tc_ref[t : t + 1, lanes] + swapped * ts_ref[t : t + 1, lanes]
                high, low = halves(y)
                rows = slice(t * CHUNK, (t + 1) * CHUNK)
                stack_ref[0, rows, :128] = high[:, :128]
                stack_ref[0, rows, 128:] = low[:, :128]
                stack_ref[1, rows, :128] = high[:, 128:]
                stack_ref[1, rows, 128:] = low[:, 128:]
            rows = slice(steps[0] * CHUNK, (steps[-1] + 1) * CHUNK)
            for parity in range(2):
                both = dot(stack_ref[parity, rows], forward_ref[...])
                columns = pl.ds(pl.multiple_of(jp * PAIR + parity * 128, 128), 128)
                hat_ref[rows, columns] = (both[:, :128] + both[:, 128:]).astype(BF16)
        return carry

    lax.fori_loop(0, cycles // 2, transform, 0)

    columns = expo_ref.shape[1]
    both = dot(hat_ref[...], bt_ref[...], ((1,), (1,)))
    expo_ref[...] = both[:, :columns] + both[:, columns:]
    step_rows = [slice(t * CHUNK, (t + 1) * CHUNK) for t in range(STEPS)]
    top = expo_ref[step_rows[0], :]
    for rows in step_rows[1:]:
        top = jnp.maximum(top, expo_ref[rows, :])
    peak = jnp.max(top, axis=1, keepdims=True)
    total = jnp.zeros((CHUNK, columns), F32)
    for rows in step_rows:
        value = jnp.exp(expo_ref[rows, :] - peak)
        expo_ref[rows, :] = value
        total = total + value
    mass = jnp.sum(total, axis=1, keepdims=True)
    diagonal = lax.broadcasted_iota(jnp.int32, (CHUNK, 128), 0) == lax.broadcasted_iota(
        jnp.int32, (CHUNK, 128), 1
    )
    peak_row = jnp.sum(jnp.where(diagonal, peak, 0.0), axis=0, keepdims=True)
    mass_row = jnp.sum(jnp.where(diagonal, mass, 0.0), axis=0, keepdims=True)
    which = lax.broadcasted_iota(jnp.int32, (8, 128), 0)
    tile = jnp.where(which == 0, peak_row, jnp.where(which == 1, mass_row, 0.0))
    for d in range(devices):
        stats_ref[d, chunk] = tile


def score_kernel(
    cycles, slots, chunks, counts_ref, near_ref, far_ref, offset_ref, tc_ref, ts_ref, forward_ref, bt_ref,
    hat_ref, expo_ref, stats_ref, starts, plain_ref, swap_ref, stack_ref, *spare,
):
    find_starts(counts_ref, starts)
    given = (counts_ref, near_ref, far_ref, offset_ref, tc_ref, ts_ref, forward_ref, bt_ref)
    held = (stats_ref, starts, plain_ref, swap_ref, stack_ref)
    if chunks == 1:
        score_chunk(cycles, slots, 0, *given, hat_ref, expo_ref, *held)
        return
    hat_now, expo_now = spare

    def body(chunk, carry):
        score_chunk(cycles, slots, chunk, *given, hat_now, expo_now, *held)
        pltpu.sync_copy(hat_now, hat_ref.at[chunk])
        pltpu.sync_copy(expo_now, expo_ref.at[chunk])
        return carry

    lax.fori_loop(0, chunks, body, 0)


def local_scores(near, far, counts, spectra, cycles, slots, chunks):
    devices = counts.shape[0]
    columns = spectra.shape[0] // 2
    tc, ts = step_tables(cycles)
    table = offset_table(cycles)
    vmem = pl.BlockSpec(memory_space=pltpu.VMEM)
    hat, expo = (ROWS, cycles * 128), (ROWS, columns)
    if chunks == 1:
        kept = (pltpu.VMEM(hat, BF16), pltpu.VMEM(expo, F32))
        place, spare = vmem, []
    else:
        kept = (
            jax.ShapeDtypeStruct((chunks, *hat), BF16),
            jax.ShapeDtypeStruct((chunks, *expo), F32),
        )
        place, spare = pl.BlockSpec(memory_space=pl.ANY), [pltpu.VMEM(hat, BF16), pltpu.VMEM(expo, F32)]
    return pl.pallas_call(
        functools.partial(score_kernel, cycles, slots, chunks),
        out_shape=(*kept, jax.ShapeDtypeStruct((devices, chunks, 8, 128), F32)),
        in_specs=[pl.BlockSpec(memory_space=pltpu.SMEM)] + [vmem] * 7,
        out_specs=(place, place, vmem),
        scratch_shapes=[
            pltpu.SMEM((devices,), jnp.int32),
            pltpu.VMEM((cycles // 2, CHUNK, PAIR), F32),
            pltpu.VMEM((cycles // 2, CHUNK, PAIR), F32),
            pltpu.VMEM((2, ROWS, 256), BF16),
            *spare,
        ],
        compiler_params=pltpu.CompilerParams(vmem_limit_bytes=(16 if chunks == 1 else 40) * MIB),
        name="local_scores",
    )(
        counts, near, far, jnp.asarray(table), jnp.asarray(tc), jnp.asarray(ts), jnp.asarray(forward_stack()),
        pltpu.with_memory_space_constraint(spectra, pltpu.VMEM),
    )


def sum_chunk(
    classes, chunk, counts_ref, stats_ref, expo_ref, hat_ref, cos_ref, sin_ref, loglik_ref, weight_ref, sums_ref,
):
    slots = loglik_ref.shape[1]
    me = lax.axis_index("blk")
    columns = classes * ANGLES
    peaks = stats_ref[:, chunk, 0, :]
    masses = stats_ref[:, chunk, 1, :]
    own_peak = stats_ref[pl.ds(me, 1), chunk, 0, :]
    peak = jnp.max(peaks, axis=0, keepdims=True)
    loglik = peak + jnp.log(jnp.sum(masses * jnp.exp(peaks - peak), axis=0, keepdims=True))
    diagonal = lax.broadcasted_iota(jnp.int32, (CHUNK, 128), 0) == lax.broadcasted_iota(
        jnp.int32, (CHUNK, 128), 1
    )
    column = lambda r: jnp.sum(jnp.where(diagonal, r, 0.0), axis=1, keepdims=True)
    scale = column(jnp.exp(own_peak - loglik))

    def add_start(d, total):
        return total + jnp.where(d < me, counts_ref[d], 0)

    start = lax.fori_loop(0, counts_ref.shape[0], add_start, jnp.int32(0))
    rank = lax.broadcasted_iota(jnp.int32, (CHUNK, slots), 0) + chunk * CHUNK
    slot = lax.broadcasted_iota(jnp.int32, (CHUNK, slots), 1)
    mine = (rank == slot + start) & (slot < counts_ref[me])
    loglik_ref[...] += jnp.sum(jnp.where(mine, column(loglik), 0.0), axis=0, keepdims=True)

    repeated = jnp.concatenate([scale] * 8, axis=0)

    def weigh(value, width, at):
        high, low = halves(value.T)
        weight_ref[:, at : at + width] = high[:, :width]

    for block in range(ROWS // 384):
        value = expo_ref[block * 384 : (block + 1) * 384, :] * repeated
        for part in range(3):
            weigh(value[part * 128 : (part + 1) * 128], 128, block * 384 + part * 128)
    rest = ROWS % 384
    if rest:
        at = ROWS - rest
        value = expo_ref[at:, :] * repeated[:rest]
        value = jnp.concatenate([value, jnp.zeros((128 - rest, columns), F32)], axis=0)
        weigh(value, rest, at)

    first = lax.broadcasted_iota(jnp.int32, (1, 128), 1) < 64
    height = sums_ref.shape[1]

    def body(i, carry):
        lanes = pl.ds(pl.multiple_of(i * (WIDE * PAIR), WIDE * PAIR), WIDE * PAIR)
        both = dot(weight_ref[...], hat_ref[:, lanes])
        totals = both
        for q in range(WIDE):
            turn_back(i * WIDE + q, totals[:, q * PAIR : (q + 1) * PAIR])
        return carry

    def turn_back(jp, total):
        rows = []
        for c in range(classes):
            block = total[c * ANGLES : (c + 1) * ANGLES]
            even = jnp.sum(block * cos_ref[...], axis=0, keepdims=True)
            odd = jnp.sum(block * sin_ref[...], axis=0, keepdims=True)
            parts = []
            for parity in range(2):
                part = slice(parity * 128, parity * 128 + 128)
                turned = pltpu.roll(odd[:, part], 64, 1)
                parts.append(even[:, part] + jnp.where(first, -turned, turned))
            rows.append(jnp.concatenate(parts, axis=1))
        if height > classes:
            rows.append(jnp.zeros((height - classes, PAIR), F32))
        sums_ref[jp] += jnp.concatenate(rows, axis=0)

    lax.fori_loop(0, sums_ref.shape[0] // WIDE, body, 0)


def sum_kernel(
    classes, chunks, counts_ref, stats_ref, expo_ref, hat_ref, cos_ref, sin_ref, image_ref, loglik_ref, out_ref,
    weight_ref, sums_ref, *spare,
):
    loglik_ref[...] = jnp.zeros_like(loglik_ref)
    sums_ref[...] = jnp.zeros_like(sums_ref)
    tables = (cos_ref, sin_ref, loglik_ref, weight_ref, sums_ref)
    if chunks == 1:
        sum_chunk(classes, 0, counts_ref, stats_ref, expo_ref, hat_ref, *tables)
    else:
        hat_now, expo_now = spare

        def body(chunk, carry):
            pltpu.sync_copy(hat_ref.at[chunk], hat_now)
            pltpu.sync_copy(expo_ref.at[chunk], expo_now)
            sum_chunk(classes, chunk, counts_ref, stats_ref, expo_now, hat_now, *tables)
            return carry

        lax.fori_loop(0, chunks, body, 0)

    height = sums_ref.shape[1]
    high, low = halves(sums_ref[...].reshape(-1, PAIR))
    upper = dot(high, image_ref[...])
    image = upper[:, :PAIR] + (upper[:, PAIR:] + dot(low, image_ref[:, :PAIR]))
    for q in range(sums_ref.shape[0]):
        for e in range(2):
            out_ref[:, e, q * 128 : (q + 1) * 128] = image[
                q * height : q * height + classes, e * 128 : (e + 1) * 128
            ]


def local_sums(counts, stats, expo, hat, classes, cycles, slots, chunks):
    columns = classes * ANGLES
    pairs = cycles // 2
    cosine, sine = gather_tables()
    vmem = pl.BlockSpec(memory_space=pltpu.VMEM)
    place, spare = vmem, []
    if chunks > 1:
        place = pl.BlockSpec(memory_space=pl.ANY)
        spare = [pltpu.VMEM((ROWS, cycles * 128), BF16), pltpu.VMEM((ROWS, columns), F32)]
    return pl.pallas_call(
        functools.partial(sum_kernel, classes, chunks),
        out_shape=(
            jax.ShapeDtypeStruct((1, slots), F32),
            jax.ShapeDtypeStruct((classes, 2, cycles * ANGLES), F32),
        ),
        in_specs=[pl.BlockSpec(memory_space=pltpu.SMEM), vmem, place, place, vmem, vmem, vmem],
        out_specs=(vmem, vmem),
        scratch_shapes=[
            pltpu.VMEM((columns, ROWS), BF16),
            pltpu.VMEM((pairs, -(-classes // 8) * 8, PAIR), F32),
            *spare,
        ],
        compiler_params=pltpu.CompilerParams(vmem_limit_bytes=(16 if chunks == 1 else 40) * MIB),
        name="local_sums",
    )(counts, stats, expo, hat, jnp.asarray(cosine), jnp.asarray(sine), jnp.asarray(image_stack()))


def local(particles, offsets, references, inv_noise, counts):
    devices = lax.axis_size("blk")
    slots = particles.shape[0]
    cycles = particles.shape[2] // ANGLES
    chunks = MEAN * devices // CHUNK
    classes = references.shape[0]
    packed = pack(particles, offsets)
    distance = devices // 2
    while True:
        if distance == 2:
            moved = lax.ppermute(packed, "blk", [(i, i ^ distance) for i in range(devices)])
            spectra = rotated_spectra(references, inv_noise, cycles)
            moved, spectra = lax.optimization_barrier((moved, spectra))
        else:
            moved = lax.ppermute(packed, "blk", [(i, i ^ distance) for i in range(devices)])
        if distance == 1:
            break
        packed = jnp.concatenate([packed, moved], axis=0)
        distance //= 2
    hat, expo, stats = local_scores(packed, moved, counts, spectra, cycles, slots, chunks)
    stats = lax.all_to_all(stats, "blk", 0, 0, tiled=True)
    loglik, class_sums = local_sums(counts, stats, expo, hat, classes, cycles, slots, chunks)
    return (loglik.reshape(slots), class_sums)


def solution(mesh):
    return jax.shard_map(
        local,
        mesh=mesh,
        in_specs=(
            P(("parts", "blk"), None, None),
            P(None, ("parts", "blk")),
            P(("parts", "blk"), None, None),
            P(),
            P("parts"),
        ),
        out_specs=(P(("parts", "blk")), P(("parts", "blk"), None, None)),
        check_vma=False,
    )
```

```python
import functools
import math

import jax
import jax.numpy as jnp
import numpy as np
from jax import lax
from jax.experimental import pallas as pl
from jax.experimental.pallas import tpu as pltpu
from jax.sharding import PartitionSpec as P

ANGLES = 64
SHIFT = 5
STEPS = SHIFT * SHIFT
MEAN = 3
CHUNK = 48
ROWS = STEPS * CHUNK
PAIR = 4 * ANGLES
WIDE = 16
STEP_GROUPS = ((0, 1, 2, 3, 4, 5, 6, 7, 8), (9, 10, 11, 12))
F32 = jnp.float32
BF16 = jnp.bfloat16
MIB = 1024 * 1024


def split(table, terms):
    rest = np.asarray(table, np.float64)
    out = []
    for _ in range(terms):
        piece = rest.astype(np.float32).astype(jnp.bfloat16)
        out.append(piece)
        rest = rest - piece.astype(np.float64)
    return out


def angle_products():
    index = np.arange(ANGLES)
    radians = 2.0 * math.pi / ANGLES * (index[:, None] * index[None, :] % ANGLES)
    return np.cos(radians), np.sin(radians)


def step_phases(cycles):
    polar = 2.0 * math.pi / ANGLES * np.arange(ANGLES)
    radius = np.arange(1, cycles + 1)
    step = np.arange(STEPS)
    along = (step // SHIFT - SHIFT // 2)[:, None] * np.cos(polar) + (step % SHIFT - SHIFT // 2)[
        :, None
    ] * np.sin(polar)
    phases = 2.0 * math.pi / 128.0 * radius[None, :, None] * along[:, None, :]
    return np.cos(phases), np.sin(phases)


def step_tables(cycles):
    cosine, sine = step_phases(cycles)
    tc = np.concatenate([cosine, cosine], axis=2).reshape(STEPS, -1).astype(np.float32)
    ts = np.concatenate([sine, -sine], axis=2).reshape(STEPS, -1).astype(np.float32)
    return tc, ts


def offset_table(cycles):
    cosine, sine = step_phases(cycles)
    both = np.concatenate([cosine.reshape(STEPS, -1), sine.reshape(STEPS, -1)], axis=1)
    both = np.pad(both, ((0, 32 - STEPS), (0, 0)))
    return np.concatenate(split(both, 3), axis=0)


def forward_matrix():
    cosine, sine = angle_products()
    return np.block([[cosine, -sine], [sine, cosine]])


def forward_stack():
    high, low = split(forward_matrix(), 2)
    return np.block([[high, low], [high, np.zeros_like(low)]])


def rotation_tables():
    cosine, sine = angle_products()
    cosine, sine = cosine / ANGLES, sine / ANGLES
    return (
        np.concatenate([cosine, cosine], axis=1).astype(np.float32),
        np.concatenate([sine, -sine], axis=1).astype(np.float32),
    )


def gather_tables():
    cosine, sine = angle_products()
    return (
        np.concatenate([cosine] * 4, axis=1).astype(np.float32),
        np.concatenate([sine] * 4, axis=1).astype(np.float32),
    )


def image_stack():
    cosine, sine = angle_products()
    table = np.zeros((2, 2, ANGLES, 2, 2, ANGLES))
    for parity in range(2):
        table[parity, 0, :, 0, parity] = cosine / ANGLES
        table[parity, 1, :, 0, parity] = -sine / ANGLES
        table[parity, 0, :, 1, parity] = sine / ANGLES
        table[parity, 1, :, 1, parity] = cosine / ANGLES
    high, low = split(table.reshape(PAIR, PAIR), 2)
    return np.concatenate([high, low], axis=1)


def dot(left, right, dims=((1,), (0,))):
    return lax.dot_general(left, right, (dims, ((), ())), preferred_element_type=F32)


def halves(value):
    high = value.astype(BF16)
    return high, (value - high.astype(F32)).astype(BF16)


def spectra_kernel(cycles, noise_ref, refs_ref, trio_ref, cos_ref, sin_ref, bt_ref, hat_ref, swap_ref):
    classes = refs_ref.shape[0] // cycles
    raw = dot(refs_ref[...], trio_ref[...])
    hat = (raw[:, :128] + raw[:, 128:256]) + raw[:, 256:]
    hat_ref[...] = hat
    swap_ref[...] = pltpu.roll(hat, 64, 1)
    cosine, sine = cos_ref[...], sin_ref[...]
    columns = classes * ANGLES

    def body(j, carry):
        weight = noise_ref[j]
        lanes = pl.ds(pl.multiple_of(j * 128, 128), 128)
        for c in range(classes):
            row = pl.ds(c * cycles + j, 1)
            plain = (hat_ref[row, :] * weight).astype(BF16).astype(F32)
            swapped = (swap_ref[row, :] * weight).astype(BF16).astype(F32)
            high, low = halves(plain * cosine + swapped * sine)
            bt_ref[c * ANGLES : (c + 1) * ANGLES, lanes] = high
            bt_ref[columns + c * ANGLES : columns + (c + 1) * ANGLES, lanes] = low
        return carry

    lax.fori_loop(0, cycles, body, 0)


def rotated_spectra(references, inv_noise, cycles):
    classes = references.shape[0]
    refs = references.reshape(classes, 2, cycles, ANGLES).transpose(0, 2, 1, 3)
    refs = refs.reshape(classes * cycles, 2 * ANGLES)
    trio = np.concatenate(split(forward_matrix(), 3), axis=1)
    cosine, sine = rotation_tables()
    vmem = pl.BlockSpec(memory_space=pltpu.VMEM)
    columns = 2 * classes * ANGLES
    return pl.pallas_call(
        functools.partial(spectra_kernel, cycles),
        out_shape=pltpu.VMEM((columns, cycles * 128), BF16),
        in_specs=[pl.BlockSpec(memory_space=pltpu.SMEM)] + [vmem] * 4,
        out_specs=vmem,
        scratch_shapes=[pltpu.VMEM((classes * cycles, 128), F32)] * 2,
        compiler_params=pltpu.CompilerParams(vmem_limit_bytes=16 * MIB),
        cost_estimate=pl.CostEstimate(
            flops=columns * cycles * 128 * 8, bytes_accessed=columns * cycles * 256, transcendentals=0
        ),
        name="rotated_spectra",
    )(inv_noise, refs, jnp.asarray(trio), jnp.asarray(cosine), jnp.asarray(sine))


def bit_reverse(value, bits):
    return sum(((value >> b) & 1) << (bits - 1 - b) for b in range(bits))


def pack_kernel(particles_hbm, offsets_hbm, out_ref, particles_ref, offsets_ref, sems):
    slots, span = particles_ref.shape[0], particles_ref.shape[2]
    copies = [
        pltpu.make_async_copy(particles_hbm, particles_ref, sems.at[0]),
        pltpu.make_async_copy(offsets_hbm, offsets_ref, sems.at[1]),
    ]
    for copy in copies:
        copy.start()
    for copy in copies:
        copy.wait()
    values = particles_ref[...].astype(F32)
    out_ref[:, :span] = values[:, 0, :].astype(BF16)
    out_ref[:, span : 2 * span] = values[:, 1, :].astype(BF16)
    offsets = offsets_ref[...].astype(F32)
    diagonal = lax.broadcasted_iota(jnp.int32, (slots, slots), 0) == lax.broadcasted_iota(
        jnp.int32, (slots, slots), 1
    )
    lane = lax.broadcasted_iota(jnp.int32, (slots, 128), 1)
    tail = jnp.zeros((slots, 128), F32)
    for axis in range(2):
        column = jnp.sum(jnp.where(diagonal, offsets[axis : axis + 1], 0.0), axis=1, keepdims=True)
        tail = jnp.where(lane == axis, column, tail)
    out_ref[:, 2 * span :] = tail.astype(BF16)


def pack(particles, offsets):
    slots, _, span = particles.shape
    vmem = pl.BlockSpec(memory_space=pltpu.VMEM)
    return pl.pallas_call(
        pack_kernel,
        out_shape=pltpu.VMEM((slots, 2 * span + 128), BF16),
        in_specs=[pl.BlockSpec(memory_space=pltpu.HBM)] * 2,
        out_specs=vmem,
        scratch_shapes=[
            pltpu.VMEM(particles.shape, particles.dtype),
            pltpu.VMEM(offsets.shape, offsets.dtype),
            pltpu.SemaphoreType.DMA((2,)),
        ],
        compiler_params=pltpu.CompilerParams(vmem_limit_bytes=2 * 1024 * 1024),
        name="pack",
    )(
        pltpu.with_memory_space_constraint(particles, pltpu.HBM),
        pltpu.with_memory_space_constraint(offsets, pltpu.HBM),
    )


def find_starts(counts_ref, starts):
    def add_start(d, total):
        starts[d] = total
        return total + counts_ref[d]

    lax.fori_loop(0, counts_ref.shape[0], add_start, jnp.int32(0))


def score_chunk(
    cycles, slots, chunk, counts_ref, near_ref, far_ref, offset_ref, tc_ref, ts_ref, forward_ref, bt_ref,
    hat_ref, expo_ref, stats_ref, starts, plain_ref, swap_ref, stack_ref,
):
    devices = counts_ref.shape[0]
    bits = devices.bit_length() - 1
    me = lax.axis_index("blk")
    width = devices // 2 * slots
    lane = lax.broadcasted_iota(jnp.int32, (1, width), 1)
    place = lane % slots
    chosen = None
    for flip, ref in ((0, near_ref), (1, far_ref)):
        rank = jnp.full((1, width), -1, jnp.int32)
        for k in range(devices // 2):
            owner = me ^ (bit_reverse(k, bits) | flip)
            here = (lane // slots == k) & (place < counts_ref[owner])
            rank = jnp.where(here, starts[owner] + place, rank)
        wanted = lax.broadcasted_iota(jnp.int32, (CHUNK, width), 0) + chunk * CHUNK
        pick = (jnp.broadcast_to(rank, (CHUNK, width)) == wanted).astype(F32).astype(BF16)
        term = dot(pick, ref[...])
        chosen = term if chosen is None else chosen + term

    span = cycles * ANGLES
    offset_x = chosen[:, 2 * span : 2 * span + 1]
    offset_y = chosen[:, 2 * span + 1 : 2 * span + 2]
    index = (offset_x + SHIFT // 2) * SHIFT + (offset_y + SHIFT // 2)
    row = lax.broadcasted_iota(jnp.int32, (CHUNK, 96), 1) % 32
    pick = (row.astype(F32) == jnp.broadcast_to(index, (CHUNK, 96))).astype(F32).astype(BF16)
    first = lax.broadcasted_iota(jnp.int32, (CHUNK, 128), 1) < 64
    for jp in range(cycles // 2):
        lanes = slice(jp * 128, jp * 128 + 128)
        cosine = dot(pick, offset_ref[:, lanes])
        sine = dot(pick, offset_ref[:, span + jp * 128 : span + jp * 128 + 128])
        real_in, imag_in = chosen[:, lanes], chosen[:, span + jp * 128 : span + jp * 128 + 128]
        real = real_in * cosine + imag_in * sine
        imag = imag_in * cosine - real_in * sine
        real_roll, imag_roll = pltpu.roll(real, 64, 1), pltpu.roll(imag, 64, 1)
        plain_ref[jp, :, :128] = jnp.where(first, real, imag_roll)
        plain_ref[jp, :, 128:] = jnp.where(first, real_roll, imag)
        swap_ref[jp, :, :128] = jnp.where(first, imag, real_roll)
        swap_ref[jp, :, 128:] = jnp.where(first, imag_roll, real)

    def transform(jp, carry):
        lanes = pl.ds(pl.multiple_of(jp * PAIR, PAIR), PAIR)
        plain, swapped = plain_ref[jp], swap_ref[jp]
        base = 0
        for steps in STEP_GROUPS:
            pieces = [(plain, tc_ref, t) for t in steps]
            pieces += [(swapped, ts_ref, t) for t in steps if t != STEPS // 2]
            for i, (value, table_ref, t) in enumerate(pieces):
                high, low = halves(value * table_ref[t : t + 1, lanes])
                rows = slice(base + i * CHUNK, base + (i + 1) * CHUNK)
                stack_ref[0, rows, :128] = high[:, :128]
                stack_ref[0, rows, 128:] = low[:, :128]
                stack_ref[1, rows, :128] = high[:, 128:]
                stack_ref[1, rows, 128:] = low[:, 128:]
            for parity in range(2):
                both = dot(stack_ref[parity, base : base + len(pieces) * CHUNK], forward_ref[...])
                whole = both[:, :128] + both[:, 128:]
                columns = pl.ds(pl.multiple_of(jp * PAIR + parity * 128, 128), 128)
                for i, t in enumerate(steps):
                    even = whole[i * CHUNK : (i + 1) * CHUNK]
                    mirror = STEPS - 1 - t
                    if mirror == t:
                        hat_ref[t * CHUNK : (t + 1) * CHUNK, columns] = even.astype(BF16)
                        continue
                    at = (len(steps) + i) * CHUNK
                    odd = whole[at : at + CHUNK]
                    hat_ref[t * CHUNK : (t + 1) * CHUNK, columns] = (even + odd).astype(BF16)
                    hat_ref[mirror * CHUNK : (mirror + 1) * CHUNK, columns] = (even - odd).astype(BF16)
            base += len(pieces) * CHUNK
        return carry

    lax.fori_loop(0, cycles // 2, transform, 0)

    columns = expo_ref.shape[1]
    both = dot(hat_ref[...], bt_ref[...], ((1,), (1,)))
    expo_ref[...] = both[:, :columns] + both[:, columns:]
    step_rows = [slice(t * CHUNK, (t + 1) * CHUNK) for t in range(STEPS)]
    top = expo_ref[step_rows[0], :]
    for rows in step_rows[1:]:
        top = jnp.maximum(top, expo_ref[rows, :])
    peak = jnp.max(top, axis=1, keepdims=True)
    total = jnp.zeros((CHUNK, columns), F32)
    for rows in step_rows:
        value = jnp.exp(expo_ref[rows, :] - peak)
        expo_ref[rows, :] = value
        total = total + value
    mass = jnp.sum(total, axis=1, keepdims=True)
    diagonal = lax.broadcasted_iota(jnp.int32, (CHUNK, 128), 0) == lax.broadcasted_iota(
        jnp.int32, (CHUNK, 128), 1
    )
    peak_row = jnp.sum(jnp.where(diagonal, peak, 0.0), axis=0, keepdims=True)
    mass_row = jnp.sum(jnp.where(diagonal, mass, 0.0), axis=0, keepdims=True)
    which = lax.broadcasted_iota(jnp.int32, (8, 128), 0)
    tile = jnp.where(which == 0, peak_row, jnp.where(which == 1, mass_row, 0.0))
    for d in range(devices):
        stats_ref[d, chunk] = tile


def score_kernel(
    cycles, slots, chunks, counts_ref, near_ref, far_ref, offset_ref, tc_ref, ts_ref, forward_ref, bt_ref,
    hat_ref, expo_ref, stats_ref, starts, plain_ref, swap_ref, stack_ref, *spare,
):
    find_starts(counts_ref, starts)
    given = (counts_ref, near_ref, far_ref, offset_ref, tc_ref, ts_ref, forward_ref, bt_ref)
    held = (stats_ref, starts, plain_ref, swap_ref, stack_ref)
    if chunks == 1:
        score_chunk(cycles, slots, 0, *given, hat_ref, expo_ref, *held)
        return
    hat_now, expo_now = spare

    def body(chunk, carry):
        score_chunk(cycles, slots, chunk, *given, hat_now, expo_now, *held)
        pltpu.sync_copy(hat_now, hat_ref.at[chunk])
        pltpu.sync_copy(expo_now, expo_ref.at[chunk])
        return carry

    lax.fori_loop(0, chunks, body, 0)


def local_scores(near, far, counts, spectra, cycles, slots, chunks):
    devices = counts.shape[0]
    columns = spectra.shape[0] // 2
    tc, ts = step_tables(cycles)
    table = offset_table(cycles)
    vmem = pl.BlockSpec(memory_space=pltpu.VMEM)
    hat, expo = (ROWS, cycles * 128), (ROWS, columns)
    if chunks == 1:
        kept = (pltpu.VMEM(hat, BF16), pltpu.VMEM(expo, F32))
        place, spare = vmem, []
    else:
        kept = (
            jax.ShapeDtypeStruct((chunks, *hat), BF16),
            jax.ShapeDtypeStruct((chunks, *expo), F32),
        )
        place, spare = pl.BlockSpec(memory_space=pl.ANY), [pltpu.VMEM(hat, BF16), pltpu.VMEM(expo, F32)]
    return pl.pallas_call(
        functools.partial(score_kernel, cycles, slots, chunks),
        out_shape=(*kept, jax.ShapeDtypeStruct((devices, chunks, 8, 128), F32)),
        in_specs=[pl.BlockSpec(memory_space=pltpu.SMEM)] + [vmem] * 7,
        out_specs=(place, place, vmem),
        scratch_shapes=[
            pltpu.SMEM((devices,), jnp.int32),
            pltpu.VMEM((cycles // 2, CHUNK, PAIR), F32),
            pltpu.VMEM((cycles // 2, CHUNK, PAIR), F32),
            pltpu.VMEM((2, ROWS, 256), BF16),
            *spare,
        ],
        compiler_params=pltpu.CompilerParams(vmem_limit_bytes=(16 if chunks == 1 else 40) * MIB),
        name="local_scores",
    )(
        counts, near, far, jnp.asarray(table), jnp.asarray(tc), jnp.asarray(ts), jnp.asarray(forward_stack()),
        pltpu.with_memory_space_constraint(spectra, pltpu.VMEM),
    )


def sum_chunk(
    classes, chunk, counts_ref, stats_ref, expo_ref, hat_ref, cos_ref, sin_ref, loglik_ref, weight_ref, sums_ref,
):
    slots = loglik_ref.shape[1]
    me = lax.axis_index("blk")
    columns = classes * ANGLES
    peaks = stats_ref[:, chunk, 0, :]
    masses = stats_ref[:, chunk, 1, :]
    own_peak = stats_ref[pl.ds(me, 1), chunk, 0, :]
    peak = jnp.max(peaks, axis=0, keepdims=True)
    loglik = peak + jnp.log(jnp.sum(masses * jnp.exp(peaks - peak), axis=0, keepdims=True))
    diagonal = lax.broadcasted_iota(jnp.int32, (CHUNK, 128), 0) == lax.broadcasted_iota(
        jnp.int32, (CHUNK, 128), 1
    )
    column = lambda r: jnp.sum(jnp.where(diagonal, r, 0.0), axis=1, keepdims=True)
    scale = column(jnp.exp(own_peak - loglik))

    def add_start(d, total):
        return total + jnp.where(d < me, counts_ref[d], 0)

    start = lax.fori_loop(0, counts_ref.shape[0], add_start, jnp.int32(0))
    rank = lax.broadcasted_iota(jnp.int32, (CHUNK, slots), 0) + chunk * CHUNK
    slot = lax.broadcasted_iota(jnp.int32, (CHUNK, slots), 1)
    mine = (rank == slot + start) & (slot < counts_ref[me])
    loglik_ref[...] += jnp.sum(jnp.where(mine, column(loglik), 0.0), axis=0, keepdims=True)

    repeated = jnp.concatenate([scale] * 8, axis=0)

    def weigh(value, width, at):
        high, low = halves(value.T)
        weight_ref[:, at : at + width] = high[:, :width]

    for block in range(ROWS // 384):
        value = expo_ref[block * 384 : (block + 1) * 384, :] * repeated
        for part in range(3):
            weigh(value[part * 128 : (part + 1) * 128], 128, block * 384 + part * 128)
    rest = ROWS % 384
    if rest:
        at = ROWS - rest
        value = expo_ref[at:, :] * repeated[:rest]
        value = jnp.concatenate([value, jnp.zeros((128 - rest, columns), F32)], axis=0)
        weigh(value, rest, at)

    first = lax.broadcasted_iota(jnp.int32, (1, 128), 1) < 64
    height = sums_ref.shape[1]

    def body(i, carry):
        lanes = pl.ds(pl.multiple_of(i * (WIDE * PAIR), WIDE * PAIR), WIDE * PAIR)
        both = dot(weight_ref[...], hat_ref[:, lanes])
        totals = both
        for q in range(WIDE):
            turn_back(i * WIDE + q, totals[:, q * PAIR : (q + 1) * PAIR])
        return carry

    def turn_back(jp, total):
        rows = []
        for c in range(classes):
            block = total[c * ANGLES : (c + 1) * ANGLES]
            even = jnp.sum(block * cos_ref[...], axis=0, keepdims=True)
            odd = jnp.sum(block * sin_ref[...], axis=0, keepdims=True)
            parts = []
            for parity in range(2):
                part = slice(parity * 128, parity * 128 + 128)
                turned = pltpu.roll(odd[:, part], 64, 1)
                parts.append(even[:, part] + jnp.where(first, -turned, turned))
            rows.append(jnp.concatenate(parts, axis=1))
        if height > classes:
            rows.append(jnp.zeros((height - classes, PAIR), F32))
        sums_ref[jp] += jnp.concatenate(rows, axis=0)

    lax.fori_loop(0, sums_ref.shape[0] // WIDE, body, 0)


def sum_kernel(
    classes, chunks, counts_ref, stats_ref, expo_ref, hat_ref, cos_ref, sin_ref, image_ref, loglik_ref, out_ref,
    weight_ref, sums_ref, *spare,
):
    loglik_ref[...] = jnp.zeros_like(loglik_ref)
    sums_ref[...] = jnp.zeros_like(sums_ref)
    tables = (cos_ref, sin_ref, loglik_ref, weight_ref, sums_ref)
    if chunks == 1:
        sum_chunk(classes, 0, counts_ref, stats_ref, expo_ref, hat_ref, *tables)
    else:
        hat_now, expo_now = spare

        def body(chunk, carry):
            pltpu.sync_copy(hat_ref.at[chunk], hat_now)
            pltpu.sync_copy(expo_ref.at[chunk], expo_now)
            sum_chunk(classes, chunk, counts_ref, stats_ref, expo_now, hat_now, *tables)
            return carry

        lax.fori_loop(0, chunks, body, 0)

    height = sums_ref.shape[1]
    high, low = halves(sums_ref[...].reshape(-1, PAIR))
    upper = dot(high, image_ref[...])
    image = upper[:, :PAIR] + (upper[:, PAIR:] + dot(low, image_ref[:, :PAIR]))
    for q in range(sums_ref.shape[0]):
        for e in range(2):
            out_ref[:, e, q * 128 : (q + 1) * 128] = image[
                q * height : q * height + classes, e * 128 : (e + 1) * 128
            ]


def local_sums(counts, stats, expo, hat, classes, cycles, slots, chunks):
    columns = classes * ANGLES
    pairs = cycles // 2
    cosine, sine = gather_tables()
    vmem = pl.BlockSpec(memory_space=pltpu.VMEM)
    place, spare = vmem, []
    if chunks > 1:
        place = pl.BlockSpec(memory_space=pl.ANY)
        spare = [pltpu.VMEM((ROWS, cycles * 128), BF16), pltpu.VMEM((ROWS, columns), F32)]
    return pl.pallas_call(
        functools.partial(sum_kernel, classes, chunks),
        out_shape=(
            jax.ShapeDtypeStruct((1, slots), F32),
            jax.ShapeDtypeStruct((classes, 2, cycles * ANGLES), F32),
        ),
        in_specs=[pl.BlockSpec(memory_space=pltpu.SMEM), vmem, place, place, vmem, vmem, vmem],
        out_specs=(vmem, vmem),
        scratch_shapes=[
            pltpu.VMEM((columns, ROWS), BF16),
            pltpu.VMEM((pairs, -(-classes // 8) * 8, PAIR), F32),
            *spare,
        ],
        compiler_params=pltpu.CompilerParams(vmem_limit_bytes=(16 if chunks == 1 else 40) * MIB),
        name="local_sums",
    )(counts, stats, expo, hat, jnp.asarray(cosine), jnp.asarray(sine), jnp.asarray(image_stack()))


def local(particles, offsets, references, inv_noise, counts):
    devices = lax.axis_size("blk")
    slots = particles.shape[0]
    cycles = particles.shape[2] // ANGLES
    chunks = MEAN * devices // CHUNK
    classes = references.shape[0]
    packed = pack(particles, offsets)
    distance = devices // 2
    while True:
        if distance == 2:
            moved = lax.ppermute(packed, "blk", [(i, i ^ distance) for i in range(devices)])
            spectra = rotated_spectra(references, inv_noise, cycles)
            moved, spectra = lax.optimization_barrier((moved, spectra))
        else:
            moved = lax.ppermute(packed, "blk", [(i, i ^ distance) for i in range(devices)])
        if distance == 1:
            break
        packed = jnp.concatenate([packed, moved], axis=0)
        distance //= 2
    hat, expo, stats = local_scores(packed, moved, counts, spectra, cycles, slots, chunks)
    stats = lax.all_to_all(stats, "blk", 0, 0, tiled=True)
    loglik, class_sums = local_sums(counts, stats, expo, hat, classes, cycles, slots, chunks)
    return (loglik.reshape(slots), class_sums)


def solution(mesh):
    return jax.shard_map(
        local,
        mesh=mesh,
        in_specs=(
            P(("parts", "blk"), None, None),
            P(None, ("parts", "blk")),
            P(("parts", "blk"), None, None),
            P(),
            P("parts"),
        ),
        out_specs=(P(("parts", "blk")), P(("parts", "blk"), None, None)),
        check_vma=False,
    )
```

```python
import functools
import math

import jax
import jax.numpy as jnp
import numpy as np
from jax import lax
from jax.experimental import pallas as pl
from jax.experimental.pallas import tpu as pltpu
from jax.sharding import PartitionSpec as P

ANGLES = 64
SHIFT = 5
STEPS = SHIFT * SHIFT
MEAN = 3
CHUNK = 48
ROWS = STEPS * CHUNK
PAIR = 4 * ANGLES
WIDE = 16
STEP_GROUPS = ((0, 1, 2, 3, 4, 5, 6, 7, 8), (9, 10, 11, 12))
SCORE_STEPS = (9, 8, 8)
F32 = jnp.float32
BF16 = jnp.bfloat16
MIB = 1024 * 1024


def split(table, terms):
    rest = np.asarray(table, np.float64)
    out = []
    for _ in range(terms):
        piece = rest.astype(np.float32).astype(jnp.bfloat16)
        out.append(piece)
        rest = rest - piece.astype(np.float64)
    return out


def angle_products():
    index = np.arange(ANGLES)
    radians = 2.0 * math.pi / ANGLES * (index[:, None] * index[None, :] % ANGLES)
    return np.cos(radians), np.sin(radians)


def step_phases(cycles):
    polar = 2.0 * math.pi / ANGLES * np.arange(ANGLES)
    radius = np.arange(1, cycles + 1)
    step = np.arange(STEPS)
    along = (step // SHIFT - SHIFT // 2)[:, None] * np.cos(polar) + (step % SHIFT - SHIFT // 2)[
        :, None
    ] * np.sin(polar)
    phases = 2.0 * math.pi / 128.0 * radius[None, :, None] * along[:, None, :]
    return np.cos(phases), np.sin(phases)


def step_tables(cycles):
    cosine, sine = step_phases(cycles)
    tc = np.concatenate([cosine, cosine], axis=2).reshape(STEPS, -1).astype(np.float32)
    ts = np.concatenate([sine, -sine], axis=2).reshape(STEPS, -1).astype(np.float32)
    return tc, ts


def offset_table(cycles):
    cosine, sine = step_phases(cycles)
    both = np.concatenate([cosine.reshape(STEPS, -1), sine.reshape(STEPS, -1)], axis=1)
    both = np.pad(both, ((0, 32 - STEPS), (0, 0)))
    return np.concatenate(split(both, 3), axis=0)


def forward_matrix():
    cosine, sine = angle_products()
    return np.block([[cosine, -sine], [sine, cosine]])


def forward_stack():
    high, low = split(forward_matrix(), 2)
    return np.block([[high, low], [high, np.zeros_like(low)]])


def rotation_tables():
    cosine, sine = angle_products()
    cosine, sine = cosine / ANGLES, sine / ANGLES
    return (
        np.concatenate([cosine, cosine], axis=1).astype(np.float32),
        np.concatenate([sine, -sine], axis=1).astype(np.float32),
    )


def gather_tables():
    cosine, sine = angle_products()
    return (
        np.concatenate([cosine] * 4, axis=1).astype(np.float32),
        np.concatenate([sine] * 4, axis=1).astype(np.float32),
    )


def image_stack():
    cosine, sine = angle_products()
    table = np.zeros((2, 2, ANGLES, 2, 2, ANGLES))
    for parity in range(2):
        table[parity, 0, :, 0, parity] = cosine / ANGLES
        table[parity, 1, :, 0, parity] = -sine / ANGLES
        table[parity, 0, :, 1, parity] = sine / ANGLES
        table[parity, 1, :, 1, parity] = cosine / ANGLES
    high, low = split(table.reshape(PAIR, PAIR), 2)
    return np.concatenate([high, low], axis=1)


def dot(left, right, dims=((1,), (0,))):
    return lax.dot_general(left, right, (dims, ((), ())), preferred_element_type=F32)


def halves(value):
    high = value.astype(BF16)
    return high, (value - high.astype(F32)).astype(BF16)


def spectra_kernel(cycles, noise_ref, refs_ref, trio_ref, cos_ref, sin_ref, bt_ref, hat_ref, swap_ref):
    classes = refs_ref.shape[0] // cycles
    raw = dot(refs_ref[...], trio_ref[...])
    hat = (raw[:, :128] + raw[:, 128:256]) + raw[:, 256:]
    hat_ref[...] = hat
    swap_ref[...] = pltpu.roll(hat, 64, 1)
    cosine, sine = cos_ref[...], sin_ref[...]
    columns = classes * ANGLES

    def body(j, carry):
        weight = noise_ref[j]
        lanes = pl.ds(pl.multiple_of(j * 128, 128), 128)
        for c in range(classes):
            row = pl.ds(c * cycles + j, 1)
            plain = (hat_ref[row, :] * weight).astype(BF16).astype(F32)
            swapped = (swap_ref[row, :] * weight).astype(BF16).astype(F32)
            high, low = halves(plain * cosine + swapped * sine)
            bt_ref[c * ANGLES : (c + 1) * ANGLES, lanes] = high
            bt_ref[columns + c * ANGLES : columns + (c + 1) * ANGLES, lanes] = low
        return carry

    lax.fori_loop(0, cycles, body, 0)


def rotated_spectra(references, inv_noise, cycles):
    classes = references.shape[0]
    refs = references.reshape(classes, 2, cycles, ANGLES).transpose(0, 2, 1, 3)
    refs = refs.reshape(classes * cycles, 2 * ANGLES)
    trio = np.concatenate(split(forward_matrix(), 3), axis=1)
    cosine, sine = rotation_tables()
    vmem = pl.BlockSpec(memory_space=pltpu.VMEM)
    columns = 2 * classes * ANGLES
    return pl.pallas_call(
        functools.partial(spectra_kernel, cycles),
        out_shape=pltpu.VMEM((columns, cycles * 128), BF16),
        in_specs=[pl.BlockSpec(memory_space=pltpu.SMEM)] + [vmem] * 4,
        out_specs=vmem,
        scratch_shapes=[pltpu.VMEM((classes * cycles, 128), F32)] * 2,
        compiler_params=pltpu.CompilerParams(vmem_limit_bytes=16 * MIB),
        cost_estimate=pl.CostEstimate(
            flops=columns * cycles * 128 * 8, bytes_accessed=columns * cycles * 256, transcendentals=0
        ),
        name="rotated_spectra",
    )(inv_noise, refs, jnp.asarray(trio), jnp.asarray(cosine), jnp.asarray(sine))


def bit_reverse(value, bits):
    return sum(((value >> b) & 1) << (bits - 1 - b) for b in range(bits))


def pack_kernel(particles_hbm, offsets_hbm, out_ref, particles_ref, offsets_ref, sems):
    slots, span = particles_ref.shape[0], particles_ref.shape[2]
    copies = [
        pltpu.make_async_copy(particles_hbm, particles_ref, sems.at[0]),
        pltpu.make_async_copy(offsets_hbm, offsets_ref, sems.at[1]),
    ]
    for copy in copies:
        copy.start()
    for copy in copies:
        copy.wait()
    values = particles_ref[...].astype(F32)
    out_ref[:, :span] = values[:, 0, :].astype(BF16)
    out_ref[:, span : 2 * span] = values[:, 1, :].astype(BF16)
    offsets = offsets_ref[...].astype(F32)
    diagonal = lax.broadcasted_iota(jnp.int32, (slots, slots), 0) == lax.broadcasted_iota(
        jnp.int32, (slots, slots), 1
    )
    lane = lax.broadcasted_iota(jnp.int32, (slots, 128), 1)
    tail = jnp.zeros((slots, 128), F32)
    for axis in range(2):
        column = jnp.sum(jnp.where(diagonal, offsets[axis : axis + 1], 0.0), axis=1, keepdims=True)
        tail = jnp.where(lane == axis, column, tail)
    out_ref[:, 2 * span :] = tail.astype(BF16)


def pack(particles, offsets):
    slots, _, span = particles.shape
    vmem = pl.BlockSpec(memory_space=pltpu.VMEM)
    return pl.pallas_call(
        pack_kernel,
        out_shape=pltpu.VMEM((slots, 2 * span + 128), BF16),
        in_specs=[pl.BlockSpec(memory_space=pltpu.HBM)] * 2,
        out_specs=vmem,
        scratch_shapes=[
            pltpu.VMEM(particles.shape, particles.dtype),
            pltpu.VMEM(offsets.shape, offsets.dtype),
            pltpu.SemaphoreType.DMA((2,)),
        ],
        compiler_params=pltpu.CompilerParams(vmem_limit_bytes=2 * 1024 * 1024),
        name="pack",
    )(
        pltpu.with_memory_space_constraint(particles, pltpu.HBM),
        pltpu.with_memory_space_constraint(offsets, pltpu.HBM),
    )


def find_starts(counts_ref, starts):
    def add_start(d, total):
        starts[d] = total
        return total + counts_ref[d]

    lax.fori_loop(0, counts_ref.shape[0], add_start, jnp.int32(0))


def choose(flip, slots, chunk, counts_ref, starts, ref):
    devices = counts_ref.shape[0]
    bits = devices.bit_length() - 1
    me = lax.axis_index("blk")
    width = devices // 2 * slots
    lane = lax.broadcasted_iota(jnp.int32, (1, width), 1)
    place = lane % slots
    rank = jnp.full((1, width), -1, jnp.int32)
    for k in range(devices // 2):
        owner = me ^ (bit_reverse(k, bits) | flip)
        here = (lane // slots == k) & (place < counts_ref[owner])
        rank = jnp.where(here, starts[owner] + place, rank)
    wanted = lax.broadcasted_iota(jnp.int32, (CHUNK, width), 0) + chunk * CHUNK
    pick = (jnp.broadcast_to(rank, (CHUNK, width)) == wanted).astype(F32).astype(BF16)
    return dot(pick, ref[...])


def near_kernel(slots, counts_ref, near_ref, out_ref, starts):
    find_starts(counts_ref, starts)
    out_ref[...] = choose(0, slots, 0, counts_ref, starts, near_ref)


def near_choice(near, counts, slots):
    vmem = pl.BlockSpec(memory_space=pltpu.VMEM)
    return pl.pallas_call(
        functools.partial(near_kernel, slots),
        out_shape=pltpu.VMEM((CHUNK, near.shape[1]), F32),
        in_specs=[pl.BlockSpec(memory_space=pltpu.SMEM), vmem],
        out_specs=vmem,
        scratch_shapes=[pltpu.SMEM(counts.shape, jnp.int32)],
        compiler_params=pltpu.CompilerParams(vmem_limit_bytes=8 * MIB),
        cost_estimate=pl.CostEstimate(flops=10**9, bytes_accessed=10**6, transcendentals=0),
        name="near_choice",
    )(counts, pltpu.with_memory_space_constraint(near, pltpu.VMEM))


def score_chunk(
    cycles, slots, chunk, counts_ref, near_ref, far_ref, offset_ref, tc_ref, ts_ref, forward_ref, bt_ref,
    hat_ref, expo_ref, stats_ref, starts, plain_ref, swap_ref, stack_ref,
):
    if near_ref.dtype == F32:
        chosen = near_ref[...]
    else:
        chosen = choose(0, slots, chunk, counts_ref, starts, near_ref)
    chosen = chosen + choose(1, slots, chunk, counts_ref, starts, far_ref)

    span = cycles * ANGLES
    offset_x = chosen[:, 2 * span : 2 * span + 1]
    offset_y = chosen[:, 2 * span + 1 : 2 * span + 2]
    index = (offset_x + SHIFT // 2) * SHIFT + (offset_y + SHIFT // 2)
    row = lax.broadcasted_iota(jnp.int32, (CHUNK, 96), 1) % 32
    pick = (row.astype(F32) == jnp.broadcast_to(index, (CHUNK, 96))).astype(F32).astype(BF16)
    first = lax.broadcasted_iota(jnp.int32, (CHUNK, 128), 1) < 64
    for jp in range(cycles // 2):
        lanes = slice(jp * 128, jp * 128 + 128)
        cosine = dot(pick, offset_ref[:, lanes])
        sine = dot(pick, offset_ref[:, span + jp * 128 : span + jp * 128 + 128])
        real_in, imag_in = chosen[:, lanes], chosen[:, span + jp * 128 : span + jp * 128 + 128]
        real = real_in * cosine + imag_in * sine
        imag = imag_in * cosine - real_in * sine
        real_roll, imag_roll = pltpu.roll(real, 64, 1), pltpu.roll(imag, 64, 1)
        plain_ref[jp, :, :128] = jnp.where(first, real, imag_roll)
        plain_ref[jp, :, 128:] = jnp.where(first, real_roll, imag)
        swap_ref[jp, :, :128] = jnp.where(first, imag, real_roll)
        swap_ref[jp, :, 128:] = jnp.where(first, imag_roll, real)

    def transform(jp, carry):
        lanes = pl.ds(pl.multiple_of(jp * PAIR, PAIR), PAIR)
        plain, swapped = plain_ref[jp], swap_ref[jp]
        base = 0
        for steps in STEP_GROUPS:
            pieces = [(plain, tc_ref, t) for t in steps]
            pieces += [(swapped, ts_ref, t) for t in steps if t != STEPS // 2]
            for i, (value, table_ref, t) in enumerate(pieces):
                high, low = halves(value * table_ref[t : t + 1, lanes])
                rows = slice(base + i * CHUNK, base + (i + 1) * CHUNK)
                stack_ref[0, rows, :128] = high[:, :128]
                stack_ref[0, rows, 128:] = low[:, :128]
                stack_ref[1, rows, :128] = high[:, 128:]
                stack_ref[1, rows, 128:] = low[:, 128:]
            for parity in range(2):
                both = dot(stack_ref[parity, base : base + len(pieces) * CHUNK], forward_ref[...])
                whole = both[:, :128] + both[:, 128:]
                columns = pl.ds(pl.multiple_of(jp * PAIR + parity * 128, 128), 128)
                for i, t in enumerate(steps):
                    even = whole[i * CHUNK : (i + 1) * CHUNK]
                    mirror = STEPS - 1 - t
                    if mirror == t:
                        hat_ref[t * CHUNK : (t + 1) * CHUNK, columns] = even.astype(BF16)
                        continue
                    at = (len(steps) + i) * CHUNK
                    odd = whole[at : at + CHUNK]
                    hat_ref[t * CHUNK : (t + 1) * CHUNK, columns] = (even + odd).astype(BF16)
                    hat_ref[mirror * CHUNK : (mirror + 1) * CHUNK, columns] = (even - odd).astype(BF16)
            base += len(pieces) * CHUNK
        return carry

    lax.fori_loop(0, cycles // 2, transform, 0)

    columns = expo_ref.shape[1]
    at = 0
    for steps in SCORE_STEPS:
        rows = slice(at * CHUNK, (at + steps) * CHUNK)
        both = dot(hat_ref[rows, :], bt_ref[...], ((1,), (1,)))
        expo_ref[rows, :] = both[:, :columns] + both[:, columns:]
        at += steps
    step_rows = [slice(t * CHUNK, (t + 1) * CHUNK) for t in range(STEPS)]
    top = expo_ref[step_rows[0], :]
    for rows in step_rows[1:]:
        top = jnp.maximum(top, expo_ref[rows, :])
    peak = jnp.max(top, axis=1, keepdims=True)
    total = jnp.zeros((CHUNK, columns), F32)
    for rows in step_rows:
        value = jnp.exp(expo_ref[rows, :] - peak)
        expo_ref[rows, :] = value
        total = total + value
    mass = jnp.sum(total, axis=1, keepdims=True)
    diagonal = lax.broadcasted_iota(jnp.int32, (CHUNK, 128), 0) == lax.broadcasted_iota(
        jnp.int32, (CHUNK, 128), 1
    )
    peak_row = jnp.sum(jnp.where(diagonal, peak, 0.0), axis=0, keepdims=True)
    mass_row = jnp.sum(jnp.where(diagonal, mass, 0.0), axis=0, keepdims=True)
    which = lax.broadcasted_iota(jnp.int32, (8, 128), 0)
    tile = jnp.where(which == 0, peak_row, jnp.where(which == 1, mass_row, 0.0))
    for d in range(stats_ref.shape[0]):
        stats_ref[d, chunk] = tile


def score_kernel(
    cycles, slots, chunks, counts_ref, near_ref, far_ref, offset_ref, tc_ref, ts_ref, forward_ref, bt_ref,
    hat_ref, expo_ref, stats_ref, starts, plain_ref, swap_ref, stack_ref, *spare,
):
    find_starts(counts_ref, starts)
    given = (counts_ref, near_ref, far_ref, offset_ref, tc_ref, ts_ref, forward_ref, bt_ref)
    held = (stats_ref, starts, plain_ref, swap_ref, stack_ref)
    if chunks == 1:
        score_chunk(cycles, slots, 0, *given, hat_ref, expo_ref, *held)
        return
    hat_now, expo_now = spare

    def body(chunk, carry):
        score_chunk(cycles, slots, chunk, *given, hat_now, expo_now, *held)
        pltpu.sync_copy(hat_now, hat_ref.at[chunk])
        pltpu.sync_copy(expo_now, expo_ref.at[chunk])
        return carry

    lax.fori_loop(0, chunks, body, 0)


def local_scores(near, far, counts, spectra, cycles, slots, chunks):
    devices = counts.shape[0]
    columns = spectra.shape[0] // 2
    tc, ts = step_tables(cycles)
    table = offset_table(cycles)
    vmem = pl.BlockSpec(memory_space=pltpu.VMEM)
    hat, expo = (ROWS, cycles * 128), (ROWS, columns)
    if chunks == 1:
        kept = (pltpu.VMEM(hat, BF16), pltpu.VMEM(expo, F32))
        place, spare = vmem, []
    else:
        kept = (
            jax.ShapeDtypeStruct((chunks, *hat), BF16),
            jax.ShapeDtypeStruct((chunks, *expo), F32),
        )
        place, spare = pl.BlockSpec(memory_space=pl.ANY), [pltpu.VMEM(hat, BF16), pltpu.VMEM(expo, F32)]
    return pl.pallas_call(
        functools.partial(score_kernel, cycles, slots, chunks),
        out_shape=(*kept, jax.ShapeDtypeStruct((devices, chunks, 8, 128), F32)),
        in_specs=[pl.BlockSpec(memory_space=pltpu.SMEM)] + [vmem] * 7,
        out_specs=(place, place, vmem),
        scratch_shapes=[
            pltpu.SMEM((devices,), jnp.int32),
            pltpu.VMEM((cycles // 2, CHUNK, PAIR), F32),
            pltpu.VMEM((cycles // 2, CHUNK, PAIR), F32),
            pltpu.VMEM((2, ROWS, 256), BF16),
            *spare,
        ],
        compiler_params=pltpu.CompilerParams(vmem_limit_bytes=(16 if chunks == 1 else 40) * MIB),
        name="local_scores",
    )(
        counts, near, far, jnp.asarray(table), jnp.asarray(tc), jnp.asarray(ts), jnp.asarray(forward_stack()),
        pltpu.with_memory_space_constraint(spectra, pltpu.VMEM),
    )


def sum_chunk(
    classes, chunk, counts_ref, stats_ref, expo_ref, hat_ref, cos_ref, sin_ref, loglik_ref, weight_ref, sums_ref,
):
    slots = loglik_ref.shape[1]
    me = lax.axis_index("blk")
    columns = classes * ANGLES
    peaks = stats_ref[:, chunk, 0, :]
    masses = stats_ref[:, chunk, 1, :]
    own_peak = stats_ref[pl.ds(me, 1), chunk, 0, :]
    peak = jnp.max(peaks, axis=0, keepdims=True)
    loglik = peak + jnp.log(jnp.sum(masses * jnp.exp(peaks - peak), axis=0, keepdims=True))
    diagonal = lax.broadcasted_iota(jnp.int32, (CHUNK, 128), 0) == lax.broadcasted_iota(
        jnp.int32, (CHUNK, 128), 1
    )
    column = lambda r: jnp.sum(jnp.where(diagonal, r, 0.0), axis=1, keepdims=True)
    scale = column(jnp.exp(own_peak - loglik))

    def add_start(d, total):
        return total + jnp.where(d < me, counts_ref[d], 0)

    start = lax.fori_loop(0, counts_ref.shape[0], add_start, jnp.int32(0))
    rank = lax.broadcasted_iota(jnp.int32, (CHUNK, slots), 0) + chunk * CHUNK
    slot = lax.broadcasted_iota(jnp.int32, (CHUNK, slots), 1)
    mine = (rank == slot + start) & (slot < counts_ref[me])
    loglik_ref[...] += jnp.sum(jnp.where(mine, column(loglik), 0.0), axis=0, keepdims=True)

    repeated = jnp.concatenate([scale] * 8, axis=0)

    def weigh(value, width, at):
        high, low = halves(value.T)
        weight_ref[:, at : at + width] = high[:, :width]

    for block in range(ROWS // 384):
        value = expo_ref[block * 384 : (block + 1) * 384, :] * repeated
        for part in range(3):
            weigh(value[part * 128 : (part + 1) * 128], 128, block * 384 + part * 128)
    rest = ROWS % 384
    if rest:
        at = ROWS - rest
        value = expo_ref[at:, :] * repeated[:rest]
        value = jnp.concatenate([value, jnp.zeros((128 - rest, columns), F32)], axis=0)
        weigh(value, rest, at)

    first = lax.broadcasted_iota(jnp.int32, (1, 128), 1) < 64
    height = sums_ref.shape[1]

    def body(i, carry):
        lanes = pl.ds(pl.multiple_of(i * (WIDE * PAIR), WIDE * PAIR), WIDE * PAIR)
        both = dot(weight_ref[...], hat_ref[:, lanes])
        totals = both
        for q in range(WIDE):
            turn_back(i * WIDE + q, totals[:, q * PAIR : (q + 1) * PAIR])
        return carry

    def turn_back(jp, total):
        rows = []
        for c in range(classes):
            block = total[c * ANGLES : (c + 1) * ANGLES]
            even = jnp.sum(block * cos_ref[...], axis=0, keepdims=True)
            odd = jnp.sum(block * sin_ref[...], axis=0, keepdims=True)
            parts = []
            for parity in range(2):
                part = slice(parity * 128, parity * 128 + 128)
                turned = pltpu.roll(odd[:, part], 64, 1)
                parts.append(even[:, part] + jnp.where(first, -turned, turned))
            rows.append(jnp.concatenate(parts, axis=1))
        if height > classes:
            rows.append(jnp.zeros((height - classes, PAIR), F32))
        sums_ref[jp] += jnp.concatenate(rows, axis=0)

    lax.fori_loop(0, sums_ref.shape[0] // WIDE, body, 0)


def sum_kernel(
    classes, chunks, counts_ref, stats_ref, expo_ref, hat_ref, cos_ref, sin_ref, image_ref, loglik_ref, out_ref,
    weight_ref, sums_ref, *spare,
):
    loglik_ref[...] = jnp.zeros_like(loglik_ref)
    sums_ref[...] = jnp.zeros_like(sums_ref)
    tables = (cos_ref, sin_ref, loglik_ref, weight_ref, sums_ref)
    if chunks == 1:
        sum_chunk(classes, 0, counts_ref, stats_ref, expo_ref, hat_ref, *tables)
    else:
        hat_now, expo_now = spare

        def body(chunk, carry):
            pltpu.sync_copy(hat_ref.at[chunk], hat_now)
            pltpu.sync_copy(expo_ref.at[chunk], expo_now)
            sum_chunk(classes, chunk, counts_ref, stats_ref, expo_now, hat_now, *tables)
            return carry

        lax.fori_loop(0, chunks, body, 0)

    height = sums_ref.shape[1]
    high, low = halves(sums_ref[...].reshape(-1, PAIR))
    upper = dot(high, image_ref[...])
    image = upper[:, :PAIR] + (upper[:, PAIR:] + dot(low, image_ref[:, :PAIR]))
    for q in range(sums_ref.shape[0]):
        for e in range(2):
            out_ref[:, e, q * 128 : (q + 1) * 128] = image[
                q * height : q * height + classes, e * 128 : (e + 1) * 128
            ]


def local_sums(counts, stats, expo, hat, classes, cycles, slots, chunks):
    columns = classes * ANGLES
    pairs = cycles // 2
    cosine, sine = gather_tables()
    vmem = pl.BlockSpec(memory_space=pltpu.VMEM)
    place, spare = vmem, []
    if chunks > 1:
        place = pl.BlockSpec(memory_space=pl.ANY)
        spare = [pltpu.VMEM((ROWS, cycles * 128), BF16), pltpu.VMEM((ROWS, columns), F32)]
    return pl.pallas_call(
        functools.partial(sum_kernel, classes, chunks),
        out_shape=(
            jax.ShapeDtypeStruct((1, slots), F32),
            jax.ShapeDtypeStruct((classes, 2, cycles * ANGLES), F32),
        ),
        in_specs=[pl.BlockSpec(memory_space=pltpu.SMEM), vmem, place, place, vmem, vmem, vmem],
        out_specs=(vmem, vmem),
        scratch_shapes=[
            pltpu.VMEM((columns, ROWS), BF16),
            pltpu.VMEM((pairs, -(-classes // 8) * 8, PAIR), F32),
            *spare,
        ],
        compiler_params=pltpu.CompilerParams(vmem_limit_bytes=(16 if chunks == 1 else 40) * MIB),
        name="local_sums",
    )(counts, stats, expo, hat, jnp.asarray(cosine), jnp.asarray(sine), jnp.asarray(image_stack()))


def local(particles, offsets, references, inv_noise, counts):
    devices = lax.axis_size("blk")
    slots = particles.shape[0]
    cycles = particles.shape[2] // ANGLES
    chunks = MEAN * devices // CHUNK
    classes = references.shape[0]
    packed = pack(particles, offsets)
    distance = devices // 2
    while True:
        if distance == 2:
            moved = lax.ppermute(packed, "blk", [(i, i ^ distance) for i in range(devices)])
            spectra = rotated_spectra(references, inv_noise, cycles)
            moved, spectra = lax.optimization_barrier((moved, spectra))
        else:
            moved = lax.ppermute(packed, "blk", [(i, i ^ distance) for i in range(devices)])
        if distance == 1:
            break
        packed = jnp.concatenate([packed, moved], axis=0)
        distance //= 2
    near = packed
    if chunks == 1:
        near = near_choice(packed, counts, slots)
        moved, near = lax.optimization_barrier((moved, near))
        near = pltpu.with_memory_space_constraint(near, pltpu.VMEM)
    hat, expo, stats = local_scores(near, moved, counts, spectra, cycles, slots, chunks)
    stats = lax.all_to_all(stats, "blk", 0, 0, tiled=True)
    loglik, class_sums = local_sums(counts, stats, expo, hat, classes, cycles, slots, chunks)
    return (loglik.reshape(slots), class_sums)


def solution(mesh):
    return jax.shard_map(
        local,
        mesh=mesh,
        in_specs=(
            P(("parts", "blk"), None, None),
            P(None, ("parts", "blk")),
            P(("parts", "blk"), None, None),
            P(),
            P("parts"),
        ),
        out_specs=(P(("parts", "blk")), P(("parts", "blk"), None, None)),
        check_vma=False,
    )
```
